32 devices in a mesh: gx: 8 (over z, core), gy: 4 (over y, x).
Axes of the slice: x: 2, y: 2, z: 4, core: 2. Of those that a mesh axis runs over, the one named last changes fastest.
Arguments:
- water_depth: float32 [1024, 1536], P('gx', 'gy'), may hold values from 0.3 to 3
- bed_level: float32 [1024, 1536], P('gx', 'gy'), may hold values from 0 to 2
- east_flow: float32 [1024, 1536], P('gx', 'gy'), may hold values from -4 to 4
- south_flow: float32 [1024, 1536], P('gx', 'gy'), may hold values from -4 to 4
- roughness_class: int32 [1024, 1536], P('gx', 'gy'), may hold values from 0 to 7
- wet_mask: int32 [1024, 1536], P('gx', 'gy'), may hold values 0 or 1
- soil_store: float32 [8, 1536, 128], P('gx', 'gy'), may hold values from 0.05 to 0.95
- rainfall: float32 [8, 1536, 128], P('gx', 'gy'), may hold values from 0 to 0.5
- tile_column: int32 [8, 1536, 1], P('gx', 'gy'), may hold values from 0 to 3; in each aligned block of 384 rows (0 to 383, 384 to 767, ..., all dimensions but the last counted through in order) at most 192 rows name the same one
- tile_block: int32 [8, 1536], P('gx', 'gy'), may hold values from 0 to 383
Outputs:
- new_depth: float32 [1024, 1536], P('gx', 'gy')
- new_east_flow: float32 [1024, 1536], P('gx', 'gy')
- new_south_flow: float32 [1024, 1536], P('gx', 'gy')
- new_soil: float32 [8, 1536, 128], P('gx', 'gy')
The draws below stay inside these ranges and needn't reach their ends.
Inputs may be any that keep to these rules, and one draw needn't show every extreme that they name: `tile_column`: among the 384 land blocks of one device, at most 192 name the same tile column; in some device some tile column is named by exactly 192 of them. `tile_block`: several land blocks may name the same block of a tile; some blocks are named by none.
All inputs are finite; a program needn't handle non-finite values. No bound on the sum of `wet_mask` on one device may be relied on, other than what follows from the above.
Results may differ from the reference program's by a relative error of at most 0.00002.
Values sent between devices are 32-bit elements; how exact they have to be, the bound alone decides.
A program may use at most 64 MiB of HBM per device.

```python
import math
import jax
import jax.numpy as jnp
import numpy as np

TR = 128
TC = 384
SUB = 4
LAND_DEV = 384
CAP = 192
NR = 1024
NC = 1536
N_GX = 8
N_GY = 4


def with_ends(entries, own_key, low, largest):
    dims = entries.shape
    place = [jax.random.randint(jax.random.fold_in(own_key, axis), (), 0, dims[axis]) for axis in range(len(dims))]
    entries = entries.at[tuple(place)].set(low)
    longest = dims.index(max(dims))
    place[longest] = (place[longest] + 1) % dims[longest]
    return entries.at[tuple(place)].set(largest)


def level_of(stream_key, dims, cuts, least, top_value):
    level = 1.0
    for axis_at, shards_of in cuts:
        heights = jax.random.uniform(jax.random.fold_in(jax.random.fold_in(stream_key, 6), axis_at), (shards_of,), jnp.float32, least / len(cuts), top_value / len(cuts))
        level = level * jnp.repeat(jnp.exp(heights), dims[axis_at] // shards_of).reshape((-1,) + (1,) * (len(dims) - 1 - axis_at))
    return level


def shared_out(rng, own, number, rows, number_of, top, bound, skew):
    sequence = jax.random.permutation(rng, number_of)
    heavy_load, common = load_shares(number_of, rows * top, bound, skew, True), load_shares(number_of, rows * top, bound, skew, False)
    places = jnp.arange(number_of)

    def named(tallies, turn):
        used = int((tallies > 0).sum())
        fixed = max(1, used // 4)
        shifted = fixed + (places - fixed + turn * (used - fixed)) % max(1, number_of - fixed)
        return jnp.zeros((number_of,), jnp.int32).at[sequence[jnp.where(places < fixed, places, shifted)]].set(jnp.asarray(tallies, jnp.int32))

    tallies = jnp.where(number % 4 == 0, named(heavy_load, number // 4), named(common, number - number // 4 - 1))
    mixed = jax.random.permutation(jax.random.fold_in(own, 3), number_of)
    donor, sink = mixed[0:number_of // 2 * 2:2], mixed[1:number_of // 2 * 2:2]
    slack = jnp.minimum(tallies[donor] - 1, bound - tallies[sink]) // 2
    slack = jnp.where((donor == sequence[0]) | (sink == sequence[0]) | (tallies[sink] == 0), 0, jnp.maximum(slack, 0))
    shifted = jax.random.randint(jax.random.fold_in(own, 4), (number_of // 2,), 0, 1 << 20) % (slack + 1)
    tallies = tallies.at[donor].add(-shifted).at[sink].add(shifted)
    members = jnp.searchsorted(jnp.cumsum(tallies), jnp.arange(rows * top), side="right").astype(jnp.int32)
    listing = members.reshape(top, rows).T
    listing = listing[jax.random.permutation(jax.random.fold_in(own, 1), rows)]
    turn = jax.random.randint(jax.random.fold_in(own, 2), (rows, 1), 0, top)
    return jnp.take_along_axis(listing, (jnp.arange(top)[None, :] + turn) % top, axis=1)


def load_shares(count, total, limit, slope, full):
    weights = [(1 << 20) // math.isqrt(rank ** slope) + 1 for rank in range(1, count + 1)]
    largest = limit if full else min(limit, max(-(-total // count), total * weights[0] // sum(weights)))
    least = 1 if total - largest >= count - 1 else 0
    given, surplus = [largest] + [least] * (count - 1), total - largest - least * (count - 1)
    while surplus > 0:
        free = [i for i in range(1, count) if given[i] < largest] or [i for i in range(1, count) if given[i] < limit]
        pool, left = sum([weights[i] for i in free]), surplus
        for i in free:
            addition = min(limit - given[i], max(1, left * weights[i] // pool), surplus)
            given[i] = given[i] + addition
            surplus = surplus - addition
    return np.array(given)


def noise(key, shape, width, most, pieces=(), kind=jnp.bfloat16):
    loudness = level_of(key, shape, pieces, -0.22, 0.18) if pieces else 1.0
    result = jax.random.normal(key, shape, jnp.float32) * width * loudness
    return jnp.minimum(jnp.maximum(result, -most), most).astype(kind)


def setup_inputs(seed: int = 0) -> dict:
    arg_keys = jax.random.split(jax.random.key(seed), 11)
    water_depth = jnp.clip(0.3 + 2.7 * jax.random.uniform(arg_keys[0], (NR, NC), jnp.float32) ** level_of(arg_keys[0], (NR, NC), ((0, 8), (1, 4)), -0.2, 0.2), 0.3, 3.0)
    bed_level = jnp.clip(2.0 * jax.random.uniform(arg_keys[1], (NR, NC), jnp.float32) ** level_of(arg_keys[1], (NR, NC), ((0, 8), (1, 4)), -0.2, 0.2), 0.0, 2.0)
    east_flow = noise(arg_keys[2], (NR, NC), 1.0, 4.0, ((0, 8), (1, 4)), jnp.float32)
    south_flow = noise(arg_keys[3], (NR, NC), 1.0, 4.0, ((0, 8), (1, 4)), jnp.float32)
    roughness_class = with_ends(jax.random.randint(arg_keys[4], (NR, NC), 0, 8), jax.random.fold_in(arg_keys[4], 1), 0, 7).astype(jnp.int32)
    wet_mask = with_ends((jax.random.randint(arg_keys[5], (NR, NC), 0, 8) < 7).astype(jnp.int32), jax.random.fold_in(arg_keys[5], 1), 0, 1)
    soil_store = jnp.clip(0.05 + 0.9 * jax.random.uniform(arg_keys[6], (N_GX, N_GY * LAND_DEV, 128), jnp.float32) ** level_of(arg_keys[6], (N_GX, N_GY * LAND_DEV, 128), ((0, 8), (1, 4)), -0.2, 0.2), 0.05, 0.95)
    rainfall = jnp.clip(0.5 * jax.random.uniform(arg_keys[7], (N_GX, N_GY * LAND_DEV, 128), jnp.float32) ** level_of(arg_keys[7], (N_GX, N_GY * LAND_DEV, 128), ((0, 8), (1, 4)), -0.2, 0.2), 0.0, 0.5)
    tile_column_keys = jax.random.split(jax.random.fold_in(arg_keys[8], 1), N_GX * (N_GY * LAND_DEV) // LAND_DEV)
    tile_column_turns = jax.random.permutation(jax.random.fold_in(arg_keys[8], 3), N_GX * (N_GY * LAND_DEV) // LAND_DEV)
    tile_column = jax.vmap(lambda own, number: shared_out(jax.random.fold_in(arg_keys[8], 2), own, number, LAND_DEV, N_GY, 1, CAP, 2))(tile_column_keys, tile_column_turns).reshape((N_GX, N_GY * LAND_DEV, 1))
    tile_block = with_ends(jax.random.randint(arg_keys[9], (N_GX, N_GY * LAND_DEV), 0, LAND_DEV), jax.random.fold_in(arg_keys[9], 1), 0, LAND_DEV - 1).astype(jnp.int32)
    return {"water_depth": water_depth, "bed_level": bed_level, "east_flow": east_flow, "south_flow": south_flow, "roughness_class": roughness_class, "wet_mask": wet_mask, "soil_store": soil_store, "rainfall": rainfall, "tile_column": tile_column, "tile_block": tile_block}


GRAVITY = 9.81
TIME_STEP = 1.0
CELL_WIDTH = 30.0
DEPTH_FLOOR = 0.3
INFIL_RATE = 0.5
MANNING = (0.02, 0.03, 0.035, 0.045, 0.06, 0.08, 0.10, 0.15)


def roughness(roughness_class, wet_mask):
    friction = jnp.zeros(roughness_class.shape, jnp.float32)
    for class_index, coefficient in enumerate(MANNING):
        friction = jnp.where(roughness_class == class_index, coefficient * coefficient, friction)
    return jnp.where(wet_mask > 0, friction, -1.0)


def face_flow(upper_first, upper_second, base_first, base_second, fric_first, fric_second, previous):
    flow_depth = jnp.maximum(upper_first, upper_second) - jnp.maximum(base_first, base_second)
    driving = GRAVITY * TIME_STEP * jnp.maximum(flow_depth, 0.0) * (upper_second - upper_first) / CELL_WIDTH
    mean_fric = 0.5 * (jnp.maximum(fric_first, 0.0) + jnp.maximum(fric_second, 0.0))
    damping = 1.0 + GRAVITY * TIME_STEP * mean_fric * jnp.abs(previous) / jnp.maximum(flow_depth, DEPTH_FLOOR) ** (7.0 / 3.0)
    is_open = (fric_first > 0) & (fric_second > 0)
    return jnp.where(is_open, (previous - driving) / damping, 0.0)


def advance(height, eastward, southward, bottom, friction):
    surface = bottom + height
    new_east = face_flow(surface[1:-1, :-1], surface[1:-1, 1:], bottom[1:-1, :-1], bottom[1:-1, 1:],
                         friction[1:-1, :-1], friction[1:-1, 1:], eastward[1:-1, :-1])
    new_south = face_flow(surface[:-1, 1:-1], surface[1:, 1:-1], bottom[:-1, 1:-1], bottom[1:, 1:-1],
                          friction[:-1, 1:-1], friction[1:, 1:-1], southward[:-1, 1:-1])
    change = new_east[:, :-1] - new_east[:, 1:] + new_south[:-1, :] - new_south[1:, :]
    return height[1:-1, 1:-1] + (TIME_STEP / CELL_WIDTH) * change, new_east[:, 1:], new_south[1:, :]


def to_grid(blocks):
    return blocks.reshape(N_GX, N_GY, TR, TC).transpose(0, 2, 1, 3).reshape(N_GX * TR, N_GY * TC)


def to_blocks(grid):
    return grid.reshape(N_GX, TR, N_GY, TC).transpose(0, 2, 1, 3).reshape(N_GX, N_GY * LAND_DEV, 128)


def route_row(row_runoff, row_target):
    return jax.ops.segment_sum(row_runoff, row_target, num_segments=N_GY * LAND_DEV)


def pick_row(row_blocks, row_target):
    return row_blocks[row_target]


def reference(water_depth, bed_level, east_flow, south_flow, roughness_class, wet_mask, soil_store, rainfall, tile_column, tile_block):
    runoff = rainfall * soil_store * soil_store
    target = (tile_column[:, :, 0] * LAND_DEV + tile_block).astype(jnp.int32)
    inflow = jax.vmap(route_row)(runoff, target)
    friction = roughness(roughness_class, wet_mask)
    height = water_depth + to_grid(inflow)
    eastward, southward = east_flow, south_flow
    for substep in range(SUB):
        height, eastward, southward = advance(jnp.pad(height, 1), jnp.pad(eastward, 1), jnp.pad(southward, 1),
                                              jnp.pad(bed_level, 1), jnp.pad(friction, 1))
    levels = jax.vmap(pick_row)(to_blocks(height), target)
    infiltration = INFIL_RATE * (1.0 - soil_store) * (1.0 - jnp.exp(-levels))
    new_soil = soil_store + rainfall - runoff + infiltration
    return height, eastward, southward, new_soil
```

```python
import functools

import jax
import jax.numpy as jnp
from jax import lax
from jax.experimental import pallas as pl
from jax.experimental.pallas import tpu as pltpu
from jax.sharding import PartitionSpec as P

SUB = 4
GRAVITY = 9.81
TIME_STEP = 1.0
CELL_WIDTH = 30.0
DEPTH_FLOOR = 0.3
INFIL_RATE = 0.5
MANNING = (0.02, 0.03, 0.035, 0.045, 0.06, 0.08, 0.1, 0.15)
LANES = 128
EDGE = 8
MESH = pl.DeviceIdType.MESH
AROUND = ((-1, -1), (-1, 0), (-1, 1), (0, -1), (0, 1), (1, -1), (1, 0), (1, 1))
NW, N, NE, W, E, SW, S, SE = range(8)


def split3(x):
    a = x.astype(jnp.bfloat16)
    rest = x - a.astype(jnp.float32)
    b = rest.astype(jnp.bfloat16)
    c = (rest - b.astype(jnp.float32)).astype(jnp.bfloat16)
    return jnp.concatenate([a, b, c], axis=1)


def pick(mask, x):
    y = jnp.dot(mask, split3(x), preferred_element_type=jnp.float32)
    return y[:, :LANES] + y[:, LANES : 2 * LANES] + y[:, 2 * LANES :]


def east_of(x):
    return pltpu.roll(x, x.shape[1] - 1, 1)


def south_of(x):
    return pltpu.roll(x, x.shape[0] - 1, 0)


def face(eta, eta_next, base, coef, q):
    depth = jnp.maximum(eta, eta_next) - base
    driving = (GRAVITY * TIME_STEP / CELL_WIDTH) * jnp.maximum(depth, 0.0) * (eta_next - eta)
    power = jnp.exp2(jnp.log2(jnp.maximum(depth, DEPTH_FLOOR)) * (-7.0 / 3.0))
    damping = 1.0 + coef * jnp.abs(q) * power
    return jnp.where(coef > 0.0, (q - driving) / damping, 0.0)


def kernel(
    nx, ny, cap,
    depth_in, bed_in, east_in, south_in, rough_in, wet_in, soil_in, rain_in, col_in, blk_in,
    depth_out, east_out, south_out, soil_out,
    h, bed, qe, qs, fric, rough, wet, soil, rain, col, blk, newsoil,
    base_e, base_s, coef_e, coef_s,
    give, take, give_idx, take_idx, give_lev, take_lev,
    st_rows, st_cols, st_in_rows, st_in_cols, st_in_corner,
    h_rows, h_cols, h_in_rows, h_in_cols, h_in_corner,
    place, place_t, where_to, where_to_t,
    in_sem, out_sem, give_s, give_r, idx_s, idx_r, lev_s, lev_r, st_s, st_r, hs_s, hs_r,
):
    gx, gy = lax.axis_index("gx"), lax.axis_index("gy")
    tr, tc = rough.shape
    land = soil.shape[0]
    chunks = tc // LANES

    inner = (pl.ds(0, tr), pl.ds(0, tc))
    loads = [
        pltpu.make_async_copy(src, dst, in_sem.at[i])
        for i, (src, dst) in enumerate(
            [
                (col_in, col), (blk_in, blk), (soil_in, soil), (rain_in, rain),
                (rough_in, rough), (wet_in, wet), (bed_in, bed.at[inner]),
                (east_in, qe.at[inner]), (south_in, qs.at[inner]), (depth_in, h.at[inner]),
            ]
        )
    ]
    for c in loads:
        c.start()

    def there(k):
        dx, dy = AROUND[k]
        x, y = gx + dx, gy + dy
        return (x >= 0) & (x < nx) & (y >= 0) & (y < ny)

    barrier = pltpu.get_barrier_semaphore()
    for k in range(1, ny):
        pl.semaphore_signal(
            barrier, inc=1, device_id=(gx, lax.rem(gy + k, ny)), device_id_type=MESH
        )
    total = ny - 1
    for k in (NW, N, NE, SW, S, SE):
        dx, dy = AROUND[k]

        @pl.when(there(k))
        def _(dx=dx, dy=dy):
            pl.semaphore_signal(barrier, inc=1, device_id=(gx + dx, gy + dy), device_id_type=MESH)

        total = total + there(k).astype(jnp.int32)

    for k, ref in ((N, (st_in_rows, h_in_rows)), (S, (st_in_rows, h_in_rows))):
        @pl.when(jnp.logical_not(there(k)))
        def _(k=k, ref=ref):
            for r in ref:
                r[int(k == S)] = jnp.zeros(r.shape[1:], r.dtype)
    for k, ref in ((W, (st_in_cols, h_in_cols)), (E, (st_in_cols, h_in_cols))):
        @pl.when(jnp.logical_not(there(k)))
        def _(k=k, ref=ref):
            for r in ref:
                r[int(k == E)] = jnp.zeros(r.shape[1:], r.dtype)
    for n, k in enumerate((NW, NE, SW, SE)):
        @pl.when(jnp.logical_not(there(k)))
        def _(n=n):
            for r in (st_in_corner, h_in_corner):
                r[n] = jnp.zeros(r.shape[1:], r.dtype)

    loads[0].wait()
    loads[1].wait()
    column = col[...]
    groups = max(EDGE, ny)
    is_col = lax.broadcasted_iota(jnp.int32, (groups, land), 0) == column
    before = lax.broadcasted_iota(jnp.int32, (land, land), 0) < lax.broadcasted_iota(
        jnp.int32, (land, land), 1
    )
    rank = jnp.dot(
        is_col.astype(jnp.float32).astype(jnp.bfloat16),
        before.astype(jnp.float32).astype(jnp.bfloat16),
        preferred_element_type=jnp.float32,
    )
    rank = jnp.sum(jnp.where(is_col, rank, 0.0), axis=0, keepdims=True)
    slot = column.astype(jnp.float32) * cap + rank
    slots = ny * cap
    hit = lax.broadcasted_iota(jnp.int32, (slots, land), 0).astype(jnp.float32) == slot
    hit = hit.astype(jnp.float32)
    place[...] = hit.astype(jnp.bfloat16)

    block = blk[...].astype(jnp.float32)
    row = jnp.floor((block + 0.5) * (1.0 / chunks))
    chunk = block - row * chunks
    line = lax.broadcasted_iota(jnp.int32, (EDGE, land), 0)
    code = jnp.where(line == 0, row + 1.0, jnp.where(line == 1, chunk, 0.0))
    code = lax.dot_general(
        code.astype(jnp.bfloat16), place[...], (((1,), (1,)), ((), ())),
        preferred_element_type=jnp.float32,
    )
    owner = jnp.broadcast_to(code[1:2] * tr + code[0:1] - 1.0, (EDGE, slots))
    for d in range(ny):
        give_idx[d] = owner[:, d * cap : (d + 1) * cap]

    loads[2].wait()
    loads[3].wait()
    runoff = rain[...] * soil[...] * soil[...]
    packed = pick(place[...], runoff)
    for d in range(ny):
        give[d] = packed[d * cap : (d + 1) * cap]

    pl.semaphore_wait(barrier, total)

    def to_all(src, dst, ss, rs):
        out = []
        for k in range(1, ny):
            peer = lax.rem(gy + k, ny)
            out.append(
                pltpu.make_async_remote_copy(
                    src_ref=src.at[peer], dst_ref=dst.at[gy], send_sem=ss.at[k - 1],
                    recv_sem=rs.at[k - 1], device_id=(gx, peer), device_id_type=MESH,
                )
            )
        for c in out:
            c.start()
        return out

    def from_all(dst, src, ss, rs):
        for k in range(1, ny):
            peer = lax.rem(gy + ny - k, ny)
            pltpu.make_async_remote_copy(
                src_ref=src.at[peer], dst_ref=dst.at[peer], send_sem=ss.at[k - 1],
                recv_sem=rs.at[k - 1], device_id=(gx, peer), device_id_type=MESH,
            ).wait_recv()

    sent = to_all(give_idx, take_idx, idx_s, idx_r)
    sent += to_all(give, take, give_s, give_r)
    take_idx[pl.ds(gy, 1)] = give_idx[pl.ds(gy, 1)]
    take[pl.ds(gy, 1)] = give[pl.ds(gy, 1)]

    for i in range(4, 9):
        loads[i].wait()
    kind = rough[...]
    f = jnp.zeros((tr, tc), jnp.float32)
    for i, coefficient in enumerate(MANNING):
        f = jnp.where(kind == i, coefficient * coefficient, f)
    fric[inner] = jnp.where(wet[...] > 0, f, -1.0)
    lane_low = lax.broadcasted_iota(jnp.int32, (tr, LANES), 1) < LANES // 2

    def stage(fields, rows, cols):
        for i, ref in enumerate(fields):
            rows[0, i] = ref[0:EDGE, 0:tc]
            rows[1, i] = ref[tr - EDGE : tr, 0:tc]
            ends = jnp.where(lane_low, ref[0:tr, 0:LANES], ref[0:tr, tc - LANES : tc]).T
            cols[0, i] = ends[0:EDGE]
            cols[1, i] = ends[LANES - EDGE :]

    def edges(rows, cols, in_rows, in_cols, in_corner, ss, rs):
        first, last = pl.ds(0, LANES), pl.ds(tc - LANES, LANES)

        def piece(k):
            dx, dy = AROUND[k]
            if dy == 0:
                return rows.at[int(dx > 0)], in_rows.at[int(dx < 0)]
            if dx == 0:
                return cols.at[int(dy > 0)], in_cols.at[int(dy < 0)]
            side = last if dy > 0 else first
            corner = {NW: 3, NE: 2, SW: 1, SE: 0}[k]
            return rows.at[int(dx > 0), :, :, side], in_corner.at[corner]

        def copy(k):
            dx, dy = AROUND[k]
            src, dst = piece(k)
            return pltpu.make_async_remote_copy(
                src_ref=src, dst_ref=dst, send_sem=ss.at[k], recv_sem=rs.at[7 - k],
                device_id=(gx + dx, gy + dy), device_id_type=MESH,
            )

        def start():
            for k in (NW, NE, SW, SE, W, E, N, S):
                @pl.when(there(k))
                def _(k=k):
                    copy(k).start()

        def wait_recv():
            for k in range(8):
                @pl.when(there(k))
                def _(k=k):
                    copy(7 - k).wait_recv()

        def wait_send():
            for k in range(8):
                @pl.when(there(k))
                def _(k=k):
                    copy(k).wait_send()

        return start, wait_recv, wait_send

    sub_low = lax.broadcasted_iota(jnp.int32, (EDGE, 1), 0) < EDGE // 2

    def unstage(fields, in_rows, in_cols, in_corner):
        for i, ref in enumerate(fields):
            ref[tr : tr + EDGE, 0:tc] = jnp.where(sub_low, in_rows[1, i], in_rows[0, i])
            side = jnp.concatenate(
                [in_cols[1, i], jnp.zeros((LANES - 2 * EDGE, tr), jnp.float32), in_cols[0, i]],
                axis=0,
            )
            ref[0:tr, tc : tc + LANES] = side.T
            ref[tr : tr + EDGE, tc : tc + LANES] = jnp.where(
                lane_low[:EDGE],
                jnp.where(sub_low, in_corner[3, i], in_corner[1, i]),
                jnp.where(sub_low, in_corner[2, i], in_corner[0, i]),
            )

    fixed = (bed, fric, qe, qs)
    stage(fixed, st_rows, st_cols)
    st_start, st_wait, st_done = edges(
        st_rows, st_cols, st_in_rows, st_in_cols, st_in_corner, st_s, st_r
    )
    st_start()

    place_t[...] = hit.T.astype(jnp.bfloat16)

    from_all(take_idx, give_idx, idx_s, idx_r)
    ids = jnp.concatenate([take_idx[d] for d in range(ny)], axis=1)[0:1]
    target = lax.broadcasted_iota(jnp.int32, (land, slots), 0).astype(jnp.float32) == ids
    target = target.astype(jnp.float32)
    where_to[...] = target.astype(jnp.bfloat16)
    where_to_t[...] = target.T.astype(jnp.bfloat16)

    st_wait()
    unstage(fixed, st_in_rows, st_in_cols, st_in_corner)
    b, fr = bed[...], fric[...]
    b_e, f_e, b_s, f_s = east_of(b), east_of(fr), south_of(b), south_of(fr)
    half = 0.5 * GRAVITY * TIME_STEP
    base_e[...] = jnp.maximum(b, b_e)
    base_s[...] = jnp.maximum(b, b_s)
    coef_e[...] = jnp.where((fr > 0.0) & (f_e > 0.0), half * (fr + f_e), -1.0)
    coef_s[...] = jnp.where((fr > 0.0) & (f_s > 0.0), half * (fr + f_s), -1.0)

    loads[9].wait()
    from_all(take, give, give_s, give_r)
    inflow = pick(where_to[...], take[...].reshape(slots, LANES))
    for c in range(chunks):
        at = (pl.ds(0, tr), pl.ds(c * LANES, LANES))
        h[at] = h[at] + inflow[c * tr : (c + 1) * tr]

    stage((h,), h_rows, h_cols)
    h_start, h_wait, h_done = edges(
        h_rows, h_cols, h_in_rows, h_in_cols, h_in_corner, hs_s, hs_r
    )
    h_start()
    h_wait()
    unstage((h,), h_in_rows, h_in_cols, h_in_corner)

    for step in range(SUB):
        eta = h[...] + bed[...]
        e = face(eta, east_of(eta), base_e[...], coef_e[...], qe[...])
        s = face(eta, south_of(eta), base_s[...], coef_s[...], qs[...])
        qe[...] = e
        qs[...] = s
        h[...] = h[...] + (TIME_STEP / CELL_WIDTH) * (
            pltpu.roll(e, 1, 1) - e + pltpu.roll(s, 1, 0) - s
        )

    stores = [
        pltpu.make_async_copy(src.at[inner], dst, out_sem.at[i])
        for i, (src, dst) in enumerate([(h, depth_out), (qe, east_out), (qs, south_out)])
    ]
    for c in stores:
        c.start()
    blocks = jnp.concatenate(
        [h[0:tr, c * LANES : (c + 1) * LANES] for c in range(chunks)], axis=0
    )
    levels = pick(where_to_t[...], blocks)
    for d in range(ny):
        give_lev[d] = levels[d * cap : (d + 1) * cap]
    sent += to_all(give_lev, take_lev, lev_s, lev_r)
    take_lev[pl.ds(gy, 1)] = give_lev[pl.ds(gy, 1)]
    from_all(take_lev, give_lev, lev_s, lev_r)
    mine = pick(place_t[...], take_lev[...].reshape(slots, LANES))
    store = soil[...]
    runoff = rain[...] * store * store
    newsoil[...] = (
        store + rain[...] - runoff + INFIL_RATE * (1.0 - store) * (1.0 - jnp.exp(-mine))
    )
    last = pltpu.make_async_copy(newsoil, soil_out, out_sem.at[3])
    last.start()
    for c in sent:
        c.wait_send()
    st_done()
    h_done()
    for c in stores:
        c.wait()
    last.wait()


def local(depth, bed, east, south, rough, wet, soil, rain, column, block):
    nx, ny = lax.axis_size("gx"), lax.axis_size("gy")
    tr, tc = depth.shape
    land = soil.shape[1]
    cap = 2 * land // ny
    slots = ny * cap
    grid = (tr + EDGE, tc + LANES)
    f32, bf16, i32 = jnp.float32, jnp.bfloat16, jnp.int32
    v = pltpu.VMEM
    dma = pltpu.SemaphoreType.DMA
    peers = max(1, ny - 1)

    def edge_bufs(k):
        return [
            v((2, k, EDGE, tc), f32), v((2, k, EDGE, tr), f32),
            v((2, k, EDGE, tc), f32), v((2, k, EDGE, tr), f32), v((4, k, EDGE, LANES), f32),
        ]

    any_ = pl.BlockSpec(memory_space=pl.ANY)
    shape = jax.ShapeDtypeStruct
    out = pl.pallas_call(
        functools.partial(kernel, nx, ny, cap),
        out_shape=[shape((tr, tc), f32)] * 3 + [shape((land, LANES), f32)],
        in_specs=[any_] * 10,
        out_specs=[any_] * 4,
        scratch_shapes=[v(grid, f32)] * 5
        + [v((tr, tc), i32)] * 2
        + [v((land, LANES), f32)] * 2
        + [v((1, land), i32)] * 2
        + [v((land, LANES), f32)]
        + [v(grid, f32)] * 4
        + [v((ny, cap, LANES), f32)] * 2
        + [v((ny, EDGE, cap), f32)] * 2
        + [v((ny, cap, LANES), f32)] * 2
        + edge_bufs(4)
        + edge_bufs(1)
        + [v((slots, land), bf16), v((land, slots), bf16)]
        + [v((land, slots), bf16), v((slots, land), bf16)]
        + [dma((10,)), dma((4,))]
        + [dma((peers,))] * 6
        + [dma((8,))] * 4,
        compiler_params=pltpu.CompilerParams(collective_id=0, has_side_effects=True),
    )(
        depth, bed, east, south, rough, wet, soil[0], rain[0],
        column.reshape(1, land), block,
    )
    return out[0], out[1], out[2], out[3][None]


def solution(mesh):
    grid = P("gx", "gy")
    blocks = P("gx", "gy", None)
    return jax.shard_map(
        local, mesh=mesh,
        in_specs=(grid,) * 6 + (blocks,) * 3 + (grid,),
        out_specs=(grid,) * 3 + (blocks,),
        check_vma=False,
    )
```

```python
import functools

import jax
import jax.numpy as jnp
from jax import lax
from jax.experimental import pallas as pl
from jax.experimental.pallas import tpu as pltpu
from jax.sharding import PartitionSpec as P

SUB = 4
GRAVITY = 9.81
TIME_STEP = 1.0
CELL_WIDTH = 30.0
DEPTH_FLOOR = 0.3
INFIL_RATE = 0.5
MANNING = (0.02, 0.03, 0.035, 0.045, 0.06, 0.08, 0.1, 0.15)
LANES = 128
EDGE = 8
MESH = pl.DeviceIdType.MESH
AROUND = ((-1, -1), (-1, 0), (-1, 1), (0, -1), (0, 1), (1, -1), (1, 0), (1, 1))
NW, N, NE, W, E, SW, S, SE = range(8)


def split3(x):
    a = x.astype(jnp.bfloat16)
    rest = x - a.astype(jnp.float32)
    b = rest.astype(jnp.bfloat16)
    c = (rest - b.astype(jnp.float32)).astype(jnp.bfloat16)
    return jnp.concatenate([a, b, c], axis=1)


def pick(mask, x):
    y = jnp.dot(mask, split3(x), preferred_element_type=jnp.float32)
    return y[:, :LANES] + y[:, LANES : 2 * LANES] + y[:, 2 * LANES :]


def east_of(x):
    return pltpu.roll(x, x.shape[1] - 1, 1)


def south_of(x):
    return pltpu.roll(x, x.shape[0] - 1, 0)


def face(eta, eta_next, base, coef, q):
    depth = jnp.maximum(eta, eta_next) - base
    driving = (GRAVITY * TIME_STEP / CELL_WIDTH) * jnp.maximum(depth, 0.0) * (eta_next - eta)
    power = jnp.exp2(jnp.log2(jnp.maximum(depth, DEPTH_FLOOR)) * (-7.0 / 3.0))
    damping = 1.0 + coef * jnp.abs(q) * power
    return jnp.where(coef > 0.0, (q - driving) / damping, 0.0)


def kernel(
    nx, ny, cap,
    depth_in, bed_in, east_in, south_in, rough_in, wet_in, soil_in, rain_in, col_in, blk_in,
    h, qe, qs, newsoil,
    bed, fric, rough, wet, soil, rain, col, blk,
    base_e, base_s, coef_e, coef_s,
    give, take, give_idx, take_idx, give_lev, take_lev,
    st_rows, st_cols, st_in_rows, st_in_cols, st_in_corner,
    h_rows, h_cols, h_in_rows, h_in_cols, h_in_corner,
    place, place_t, where_to, where_to_t,
    in_sem, give_s, give_r, idx_s, idx_r, lev_s, lev_r, st_s, st_r, hs_s, hs_r,
):
    gx, gy = lax.axis_index("gx"), lax.axis_index("gy")
    tr, tc = rough.shape
    land = soil.shape[0]
    chunks = tc // LANES

    inner = (pl.ds(0, tr), pl.ds(0, tc))
    loads = [
        pltpu.make_async_copy(src, dst, in_sem.at[i])
        for i, (src, dst) in enumerate(
            [
                (col_in, col), (blk_in, blk), (soil_in, soil), (rain_in, rain),
                (rough_in, rough), (wet_in, wet), (bed_in, bed.at[inner]),
                (east_in, qe.at[inner]), (south_in, qs.at[inner]), (depth_in, h.at[inner]),
            ]
        )
    ]
    for c in loads:
        c.start()

    def there(k):
        dx, dy = AROUND[k]
        x, y = gx + dx, gy + dy
        return (x >= 0) & (x < nx) & (y >= 0) & (y < ny)

    barrier = pltpu.get_barrier_semaphore()
    for k in range(1, ny):
        pl.semaphore_signal(
            barrier, inc=1, device_id=(gx, lax.rem(gy + k, ny)), device_id_type=MESH
        )
    total = ny - 1
    for k in (NW, N, NE, SW, S, SE):
        dx, dy = AROUND[k]

        @pl.when(there(k))
        def _(dx=dx, dy=dy):
            pl.semaphore_signal(barrier, inc=1, device_id=(gx + dx, gy + dy), device_id_type=MESH)

        total = total + there(k).astype(jnp.int32)

    for k, ref in ((N, (st_in_rows, h_in_rows)), (S, (st_in_rows, h_in_rows))):
        @pl.when(jnp.logical_not(there(k)))
        def _(k=k, ref=ref):
            for r in ref:
                r[int(k == S)] = jnp.zeros(r.shape[1:], r.dtype)
    for k, ref in ((W, (st_in_cols, h_in_cols)), (E, (st_in_cols, h_in_cols))):
        @pl.when(jnp.logical_not(there(k)))
        def _(k=k, ref=ref):
            for r in ref:
                r[int(k == E)] = jnp.zeros(r.shape[1:], r.dtype)
    for n, k in enumerate((NW, NE, SW, SE)):
        @pl.when(jnp.logical_not(there(k)))
        def _(n=n):
            for r in (st_in_corner, h_in_corner):
                r[n] = jnp.zeros(r.shape[1:], r.dtype)

    loads[0].wait()
    loads[1].wait()
    column = col[...]
    groups = max(EDGE, ny)
    is_col = lax.broadcasted_iota(jnp.int32, (groups, land), 0) == column
    before = lax.broadcasted_iota(jnp.int32, (land, land), 0) < lax.broadcasted_iota(
        jnp.int32, (land, land), 1
    )
    rank = jnp.dot(
        is_col.astype(jnp.float32).astype(jnp.bfloat16),
        before.astype(jnp.float32).astype(jnp.bfloat16),
        preferred_element_type=jnp.float32,
    )
    rank = jnp.sum(jnp.where(is_col, rank, 0.0), axis=0, keepdims=True)
    slot = column.astype(jnp.float32) * cap + rank
    slots = ny * cap
    hit = lax.broadcasted_iota(jnp.int32, (slots, land), 0).astype(jnp.float32) == slot
    hit = hit.astype(jnp.float32)
    place[...] = hit.astype(jnp.bfloat16)

    block = blk[...].astype(jnp.float32)
    row = jnp.floor((block + 0.5) * (1.0 / chunks))
    chunk = block - row * chunks
    line = lax.broadcasted_iota(jnp.int32, (EDGE, land), 0)
    code = jnp.where(line == 0, row + 1.0, jnp.where(line == 1, chunk, 0.0))
    code = lax.dot_general(
        code.astype(jnp.bfloat16), place[...], (((1,), (1,)), ((), ())),
        preferred_element_type=jnp.float32,
    )
    owner = jnp.broadcast_to(code[1:2] * tr + code[0:1] - 1.0, (EDGE, slots))
    for d in range(ny):
        give_idx[d] = owner[:, d * cap : (d + 1) * cap]

    loads[2].wait()
    loads[3].wait()
    runoff = rain[...] * soil[...] * soil[...]
    packed = pick(place[...], runoff)
    for d in range(ny):
        give[d] = packed[d * cap : (d + 1) * cap]

    pl.semaphore_wait(barrier, total)

    def to_all(src, dst, ss, rs):
        out = []
        for k in range(1, ny):
            peer = lax.rem(gy + k, ny)
            out.append(
                pltpu.make_async_remote_copy(
                    src_ref=src.at[peer], dst_ref=dst.at[gy], send_sem=ss.at[k - 1],
                    recv_sem=rs.at[k - 1], device_id=(gx, peer), device_id_type=MESH,
                )
            )
        for c in out:
            c.start()
        return out

    def from_all(dst, src, ss, rs):
        for k in range(1, ny):
            peer = lax.rem(gy + ny - k, ny)
            pltpu.make_async_remote_copy(
                src_ref=src.at[peer], dst_ref=dst.at[peer], send_sem=ss.at[k - 1],
                recv_sem=rs.at[k - 1], device_id=(gx, peer), device_id_type=MESH,
            ).wait_recv()

    sent = to_all(give_idx, take_idx, idx_s, idx_r)
    sent += to_all(give, take, give_s, give_r)
    take_idx[pl.ds(gy, 1)] = give_idx[pl.ds(gy, 1)]
    take[pl.ds(gy, 1)] = give[pl.ds(gy, 1)]

    for i in range(4, 9):
        loads[i].wait()
    kind = rough[...]
    f = jnp.zeros((tr, tc), jnp.float32)
    for i, coefficient in enumerate(MANNING):
        f = jnp.where(kind == i, coefficient * coefficient, f)
    fric[inner] = jnp.where(wet[...] > 0, f, -1.0)
    lane_low = lax.broadcasted_iota(jnp.int32, (tr, LANES), 1) < LANES // 2

    def stage(fields, rows, cols):
        for i, ref in enumerate(fields):
            rows[0, i] = ref[0:EDGE, 0:tc]
            rows[1, i] = ref[tr - EDGE : tr, 0:tc]
            ends = jnp.where(lane_low, ref[0:tr, 0:LANES], ref[0:tr, tc - LANES : tc]).T
            cols[0, i] = ends[0:EDGE]
            cols[1, i] = ends[LANES - EDGE :]

    def edges(rows, cols, in_rows, in_cols, in_corner, ss, rs):
        first, last = pl.ds(0, LANES), pl.ds(tc - LANES, LANES)

        def piece(k):
            dx, dy = AROUND[k]
            if dy == 0:
                return rows.at[int(dx > 0)], in_rows.at[int(dx < 0)]
            if dx == 0:
                return cols.at[int(dy > 0)], in_cols.at[int(dy < 0)]
            side = last if dy > 0 else first
            corner = {NW: 3, NE: 2, SW: 1, SE: 0}[k]
            return rows.at[int(dx > 0), :, :, side], in_corner.at[corner]

        def copy(k):
            dx, dy = AROUND[k]
            src, dst = piece(k)
            return pltpu.make_async_remote_copy(
                src_ref=src, dst_ref=dst, send_sem=ss.at[k], recv_sem=rs.at[7 - k],
                device_id=(gx + dx, gy + dy), device_id_type=MESH,
            )

        def start():
            for k in (NW, NE, SW, SE, W, E, N, S):
                @pl.when(there(k))
                def _(k=k):
                    copy(k).start()

        def wait_recv():
            for k in range(8):
                @pl.when(there(k))
                def _(k=k):
                    copy(7 - k).wait_recv()

        def wait_send():
            for k in range(8):
                @pl.when(there(k))
                def _(k=k):
                    copy(k).wait_send()

        return start, wait_recv, wait_send

    sub_low = lax.broadcasted_iota(jnp.int32, (EDGE, 1), 0) < EDGE // 2

    def unstage(fields, in_rows, in_cols, in_corner):
        for i, ref in enumerate(fields):
            ref[tr : tr + EDGE, 0:tc] = jnp.where(sub_low, in_rows[1, i], in_rows[0, i])
            side = jnp.concatenate(
                [in_cols[1, i], jnp.zeros((LANES - 2 * EDGE, tr), jnp.float32), in_cols[0, i]],
                axis=0,
            )
            ref[0:tr, tc : tc + LANES] = side.T
            ref[tr : tr + EDGE, tc : tc + LANES] = jnp.where(
                lane_low[:EDGE],
                jnp.where(sub_low, in_corner[3, i], in_corner[1, i]),
                jnp.where(sub_low, in_corner[2, i], in_corner[0, i]),
            )

    fixed = (bed, fric, qe, qs)
    stage(fixed, st_rows, st_cols)
    st_start, st_wait, st_done = edges(
        st_rows, st_cols, st_in_rows, st_in_cols, st_in_corner, st_s, st_r
    )
    st_start()

    place_t[...] = hit.T.astype(jnp.bfloat16)

    from_all(take_idx, give_idx, idx_s, idx_r)
    ids = jnp.concatenate([take_idx[d] for d in range(ny)], axis=1)[0:1]
    target = lax.broadcasted_iota(jnp.int32, (land, slots), 0).astype(jnp.float32) == ids
    target = target.astype(jnp.float32)
    where_to[...] = target.astype(jnp.bfloat16)
    where_to_t[...] = target.T.astype(jnp.bfloat16)

    st_wait()
    unstage(fixed, st_in_rows, st_in_cols, st_in_corner)
    b, fr = bed[...], fric[...]
    b_e, f_e, b_s, f_s = east_of(b), east_of(fr), south_of(b), south_of(fr)
    half = 0.5 * GRAVITY * TIME_STEP
    base_e[...] = jnp.maximum(b, b_e)
    base_s[...] = jnp.maximum(b, b_s)
    coef_e[...] = jnp.where((fr > 0.0) & (f_e > 0.0), half * (fr + f_e), -1.0)
    coef_s[...] = jnp.where((fr > 0.0) & (f_s > 0.0), half * (fr + f_s), -1.0)

    loads[9].wait()
    from_all(take, give, give_s, give_r)
    inflow = pick(where_to[...], take[...].reshape(slots, LANES))
    for c in range(chunks):
        at = (pl.ds(0, tr), pl.ds(c * LANES, LANES))
        h[at] = h[at] + inflow[c * tr : (c + 1) * tr]

    stage((h,), h_rows, h_cols)
    h_start, h_wait, h_done = edges(
        h_rows, h_cols, h_in_rows, h_in_cols, h_in_corner, hs_s, hs_r
    )
    h_start()
    h_wait()
    unstage((h,), h_in_rows, h_in_cols, h_in_corner)

    for step in range(SUB):
        eta = h[...] + bed[...]
        e = face(eta, east_of(eta), base_e[...], coef_e[...], qe[...])
        s = face(eta, south_of(eta), base_s[...], coef_s[...], qs[...])
        qe[...] = e
        qs[...] = s
        h[...] = h[...] + (TIME_STEP / CELL_WIDTH) * (
            pltpu.roll(e, 1, 1) - e + pltpu.roll(s, 1, 0) - s
        )

    blocks = jnp.concatenate(
        [h[0:tr, c * LANES : (c + 1) * LANES] for c in range(chunks)], axis=0
    )
    levels = pick(where_to_t[...], blocks)
    for d in range(ny):
        give_lev[d] = levels[d * cap : (d + 1) * cap]
    sent += to_all(give_lev, take_lev, lev_s, lev_r)
    take_lev[pl.ds(gy, 1)] = give_lev[pl.ds(gy, 1)]
    from_all(take_lev, give_lev, lev_s, lev_r)
    mine = pick(place_t[...], take_lev[...].reshape(slots, LANES))
    store = soil[...]
    runoff = rain[...] * store * store
    newsoil[...] = (
        store + rain[...] - runoff + INFIL_RATE * (1.0 - store) * (1.0 - jnp.exp(-mine))
    )
    for c in sent:
        c.wait_send()
    st_done()
    h_done()


def write_out(h, qe, qs, newsoil, depth_out, east_out, south_out, soil_out, sem):
    tr, tc = depth_out.shape
    inner = (pl.ds(0, tr), pl.ds(0, tc))
    copies = [
        pltpu.make_async_copy(src, dst, sem.at[i])
        for i, (src, dst) in enumerate(
            [
                (h.at[inner], depth_out), (qe.at[inner], east_out),
                (qs.at[inner], south_out), (newsoil, soil_out),
            ]
        )
    ]
    for c in copies:
        c.start()
    for c in copies:
        c.wait()


def local(depth, bed, east, south, rough, wet, soil, rain, column, block):
    nx, ny = lax.axis_size("gx"), lax.axis_size("gy")
    tr, tc = depth.shape
    land = soil.shape[1]
    cap = 2 * land // ny
    slots = ny * cap
    grid = (tr + EDGE, tc + LANES)
    f32, bf16, i32 = jnp.float32, jnp.bfloat16, jnp.int32
    v = pltpu.VMEM
    dma = pltpu.SemaphoreType.DMA
    peers = max(1, ny - 1)

    def edge_bufs(k):
        return [
            v((2, k, EDGE, tc), f32), v((2, k, EDGE, tr), f32),
            v((2, k, EDGE, tc), f32), v((2, k, EDGE, tr), f32), v((4, k, EDGE, LANES), f32),
        ]

    any_ = pl.BlockSpec(memory_space=pltpu.MemorySpace.HBM)
    vmem = pl.BlockSpec(memory_space=pltpu.VMEM)
    shape = jax.ShapeDtypeStruct
    out = pl.pallas_call(
        functools.partial(kernel, nx, ny, cap),
        out_shape=[shape(grid, f32)] * 3 + [shape((land, LANES), f32)],
        in_specs=[any_] * 10,
        out_specs=[vmem] * 4,
        scratch_shapes=[v(grid, f32)] * 2
        + [v((tr, tc), i32)] * 2
        + [v((land, LANES), f32)] * 2
        + [v((1, land), i32)] * 2
        + [v(grid, f32)] * 4
        + [v((ny, cap, LANES), f32)] * 2
        + [v((ny, EDGE, cap), f32)] * 2
        + [v((ny, cap, LANES), f32)] * 2
        + edge_bufs(4)
        + edge_bufs(1)
        + [v((slots, land), bf16), v((land, slots), bf16)]
        + [v((land, slots), bf16), v((slots, land), bf16)]
        + [dma((10,))]
        + [dma((peers,))] * 6
        + [dma((8,))] * 4,
        compiler_params=pltpu.CompilerParams(collective_id=0, has_side_effects=True, vmem_limit_bytes=24 << 20
        ),
    )(
        *[pltpu.with_memory_space_constraint(x, pltpu.MemorySpace.HBM) for x in (depth, bed, east, south, rough, wet, soil[0], rain[0],
        column.reshape(1, land), block)]
    )
    out = pl.pallas_call(
        write_out,
        out_shape=[shape((tr, tc), f32)] * 3 + [shape((land, LANES), f32)],
        in_specs=[vmem] * 4,
        out_specs=[any_] * 4,
        scratch_shapes=[dma((4,))],
        compiler_params=pltpu.CompilerParams(vmem_limit_bytes=8 << 20),
    )(*out)
    return out[0], out[1], out[2], out[3][None]


def solution(mesh):
    grid = P("gx", "gy")
    blocks = P("gx", "gy", None)
    return jax.shard_map(
        local, mesh=mesh,
        in_specs=(grid,) * 6 + (blocks,) * 3 + (grid,),
        out_specs=(grid,) * 3 + (blocks,),
        check_vma=False,
    )
```

```python
import functools

import jax
import jax.numpy as jnp
from jax import lax
from jax.experimental import pallas as pl
from jax.experimental.pallas import tpu as pltpu
from jax.sharding import PartitionSpec as P

SUB = 4
GRAVITY = 9.81
TIME_STEP = 1.0
CELL_WIDTH = 30.0
DEPTH_FLOOR = 0.3
INFIL_RATE = 0.5
MANNING = (0.02, 0.03, 0.035, 0.045, 0.06, 0.08, 0.1, 0.15)
LANES = 128
EDGE = 8
MESH = pl.DeviceIdType.MESH
AROUND = ((-1, -1), (-1, 0), (-1, 1), (0, -1), (0, 1), (1, -1), (1, 0), (1, 1))
NW, N, NE, W, E, SW, S, SE = range(8)


def split3(x):
    a = x.astype(jnp.bfloat16)
    rest = x - a.astype(jnp.float32)
    b = rest.astype(jnp.bfloat16)
    c = (rest - b.astype(jnp.float32)).astype(jnp.bfloat16)
    return jnp.concatenate([a, b, c], axis=1)


def pick(mask, x):
    x = x if x.dtype == jnp.bfloat16 else split3(x)
    y = jnp.dot(mask, x, preferred_element_type=jnp.float32)
    return y[:, :LANES] + y[:, LANES : 2 * LANES] + y[:, 2 * LANES :]


def flip(i, k, n):
    if n & (n - 1):
        return None
    both, bit = 0, 1
    while bit < n:
        if k & bit:
            both = both + bit * lax.rem(i // bit, 2)
        bit *= 2
    return i + k - 2 * both


def offsets(n):
    return sorted(range(1, n), key=lambda k: -bin(k).count("1"))


def east_of(x):
    return pltpu.roll(x, x.shape[1] - 1, 1)


def south_of(x):
    return pltpu.roll(x, x.shape[0] - 1, 0)


def face(eta, eta_next, base, coef, q):
    depth = jnp.maximum(eta, eta_next) - base
    driving = (GRAVITY * TIME_STEP / CELL_WIDTH) * jnp.maximum(depth, 0.0) * (eta_next - eta)
    power = jnp.exp2(jnp.log2(jnp.maximum(depth, DEPTH_FLOOR)) * (-7.0 / 3.0))
    damping = 1.0 + coef * jnp.abs(q) * power
    return jnp.where(coef > 0.0, (q - driving) / damping, 0.0)


def kernel(
    nx, ny, cap,
    depth_in, bed_in, east_in, south_in, rough_in, wet_in, soil_in, rain_in, col_in, blk_in,
    h, qe, qs, newsoil,
    bed, fric, rough, wet, soil, rain, col, blk,
    base_e, base_s, coef_e, coef_s,
    give, take, give_idx, take_idx, give_lev, take_lev,
    st_rows, st_cols, st_in_rows, st_in_cols, st_in_corner,
    h_rows, h_cols, h_in_rows, h_in_cols, h_in_corner,
    place, place_t, where_to, where_to_t,
    in_sem, give_s, give_r, idx_s, idx_r, lev_s, lev_r, st_s, st_r, hs_s, hs_r,
):
    gx, gy = lax.axis_index("gx"), lax.axis_index("gy")
    tr, tc = rough.shape
    land = soil.shape[0]
    chunks = tc // LANES

    inner = (pl.ds(0, tr), pl.ds(0, tc))
    loads = [
        pltpu.make_async_copy(src, dst, in_sem.at[i])
        for i, (src, dst) in enumerate(
            [
                (col_in, col), (blk_in, blk), (soil_in, soil), (rain_in, rain),
                (rough_in, rough), (wet_in, wet), (bed_in, bed.at[inner]),
                (east_in, qe.at[inner]), (south_in, qs.at[inner]), (depth_in, h.at[inner]),
            ]
        )
    ]
    for c in loads:
        c.start()

    def there(k):
        dx, dy = AROUND[k]
        x, y = gx + dx, gy + dy
        return (x >= 0) & (x < nx) & (y >= 0) & (y < ny)

    barrier = pltpu.get_barrier_semaphore()
    for k in range(1, ny):
        pl.semaphore_signal(
            barrier, inc=1, device_id=(gx, lax.rem(gy + k, ny)), device_id_type=MESH
        )
    total = ny - 1
    for k in (NW, N, NE, SW, S, SE):
        dx, dy = AROUND[k]

        @pl.when(there(k))
        def _(dx=dx, dy=dy):
            pl.semaphore_signal(barrier, inc=1, device_id=(gx + dx, gy + dy), device_id_type=MESH)

        total = total + there(k).astype(jnp.int32)

    for k, ref in ((N, (st_in_rows, h_in_rows)), (S, (st_in_rows, h_in_rows))):
        @pl.when(jnp.logical_not(there(k)))
        def _(k=k, ref=ref):
            for r in ref:
                r[int(k == S)] = jnp.zeros(r.shape[1:], r.dtype)
    for k, ref in ((W, (st_in_cols, h_in_cols)), (E, (st_in_cols, h_in_cols))):
        @pl.when(jnp.logical_not(there(k)))
        def _(k=k, ref=ref):
            for r in ref:
                r[int(k == E)] = jnp.zeros(r.shape[1:], r.dtype)
    for n, k in enumerate((NW, NE, SW, SE)):
        @pl.when(jnp.logical_not(there(k)))
        def _(n=n):
            for r in (st_in_corner, h_in_corner):
                r[n] = jnp.zeros(r.shape[1:], r.dtype)

    loads[0].wait()
    loads[1].wait()
    column = col[...]
    groups = max(EDGE, ny)
    is_col = lax.broadcasted_iota(jnp.int32, (groups, land), 0) == column
    before = lax.broadcasted_iota(jnp.int32, (land, land), 0) < lax.broadcasted_iota(
        jnp.int32, (land, land), 1
    )
    rank = jnp.dot(
        is_col.astype(jnp.float32).astype(jnp.bfloat16),
        before.astype(jnp.float32).astype(jnp.bfloat16),
        preferred_element_type=jnp.float32,
    )
    rank = jnp.sum(jnp.where(is_col, rank, 0.0), axis=0, keepdims=True)
    slot = column.astype(jnp.float32) * cap + rank
    slots = ny * cap
    hit = lax.broadcasted_iota(jnp.int32, (slots, land), 0).astype(jnp.float32) == slot
    hit = hit.astype(jnp.float32)
    place[...] = hit.astype(jnp.bfloat16)

    block = blk[...].astype(jnp.float32)
    row = jnp.floor((block + 0.5) * (1.0 / chunks))
    chunk = block - row * chunks
    line = lax.broadcasted_iota(jnp.int32, (EDGE, land), 0)
    code = jnp.where(line == 0, row + 1.0, jnp.where(line == 1, chunk, 0.0))
    code = lax.dot_general(
        code.astype(jnp.bfloat16), place[...], (((1,), (1,)), ((), ())),
        preferred_element_type=jnp.float32,
    )
    owner = jnp.broadcast_to(code[1:2] * tr + code[0:1] - 1.0, (EDGE, slots))
    for d in range(ny):
        give_idx[d] = owner[:, d * cap : (d + 1) * cap]

    loads[2].wait()
    loads[3].wait()
    runoff = rain[...] * soil[...] * soil[...]
    packed = pick(place[...], runoff)
    for d in range(ny):
        give[d] = packed[d * cap : (d + 1) * cap]

    pl.semaphore_wait(barrier, total)

    def to_peer(k):
        peer = flip(gy, k, ny)
        return lax.rem(gy + k, ny) if peer is None else peer

    def from_peer(k):
        peer = flip(gy, k, ny)
        return lax.rem(gy + ny - k, ny) if peer is None else peer

    def send(src, dst, ss, rs, k):
        peer = to_peer(k)
        c = pltpu.make_async_remote_copy(
            src_ref=src.at[peer], dst_ref=dst.at[gy], send_sem=ss.at[k - 1],
            recv_sem=rs.at[k - 1], device_id=(gx, peer), device_id_type=MESH,
        )
        c.start()
        return c

    def to_all(src, dst, ss, rs):
        return [send(src, dst, ss, rs, k) for k in offsets(ny)]

    def receive(dst, src, ss, rs, k):
        peer = from_peer(k)
        pltpu.make_async_remote_copy(
            src_ref=src.at[peer], dst_ref=dst.at[peer], send_sem=ss.at[k - 1],
            recv_sem=rs.at[k - 1], device_id=(gx, peer), device_id_type=MESH,
        ).wait_recv()
        return peer

    def from_all(dst, src, ss, rs):
        for k in offsets(ny):
            receive(dst, src, ss, rs, k)

    sent = to_all(give_idx, take_idx, idx_s, idx_r)
    sent += to_all(give, take, give_s, give_r)
    take_idx[pl.ds(gy, 1)] = give_idx[pl.ds(gy, 1)]

    for i in range(4, 9):
        loads[i].wait()
    kind = rough[...]
    f = jnp.zeros((tr, tc), jnp.float32)
    for i, coefficient in enumerate(MANNING):
        f = jnp.where(kind == i, coefficient * coefficient, f)
    fric[inner] = jnp.where(wet[...] > 0, f, -1.0)
    lane_low = lax.broadcasted_iota(jnp.int32, (tr, LANES), 1) < LANES // 2

    def stage(fields, rows, cols):
        for i, ref in enumerate(fields):
            rows[0, i] = ref[0:EDGE, 0:tc]
            rows[1, i] = ref[tr - EDGE : tr, 0:tc]
            ends = jnp.where(lane_low, ref[0:tr, 0:LANES], ref[0:tr, tc - LANES : tc]).T
            cols[0, i] = ends[0:EDGE]
            cols[1, i] = ends[LANES - EDGE :]

    def edges(rows, cols, in_rows, in_cols, in_corner, ss, rs):
        first, last = pl.ds(0, LANES), pl.ds(tc - LANES, LANES)

        def piece(k):
            dx, dy = AROUND[k]
            if dy == 0:
                return rows.at[int(dx > 0)], in_rows.at[int(dx < 0)]
            if dx == 0:
                return cols.at[int(dy > 0)], in_cols.at[int(dy < 0)]
            side = last if dy > 0 else first
            corner = {NW: 3, NE: 2, SW: 1, SE: 0}[k]
            return rows.at[int(dx > 0), :, :, side], in_corner.at[corner]

        def copy(k):
            dx, dy = AROUND[k]
            src, dst = piece(k)
            return pltpu.make_async_remote_copy(
                src_ref=src, dst_ref=dst, send_sem=ss.at[k], recv_sem=rs.at[7 - k],
                device_id=(gx + dx, gy + dy), device_id_type=MESH,
            )

        def start():
            for k in (NW, NE, SW, SE, W, E, N, S):
                @pl.when(there(k))
                def _(k=k):
                    copy(k).start()

        def wait_recv():
            for k in range(8):
                @pl.when(there(k))
                def _(k=k):
                    copy(7 - k).wait_recv()

        def wait_send():
            for k in range(8):
                @pl.when(there(k))
                def _(k=k):
                    copy(k).wait_send()

        return start, wait_recv, wait_send

    sub_low = lax.broadcasted_iota(jnp.int32, (EDGE, 1), 0) < EDGE // 2

    def unstage(fields, in_rows, in_cols, in_corner):
        for i, ref in enumerate(fields):
            ref[tr : tr + EDGE, 0:tc] = jnp.where(sub_low, in_rows[1, i], in_rows[0, i])
            side = jnp.concatenate(
                [in_cols[1, i], jnp.zeros((LANES - 2 * EDGE, tr), jnp.float32), in_cols[0, i]],
                axis=0,
            )
            ref[0:tr, tc : tc + LANES] = side.T
            ref[tr : tr + EDGE, tc : tc + LANES] = jnp.where(
                lane_low[:EDGE],
                jnp.where(sub_low, in_corner[3, i], in_corner[1, i]),
                jnp.where(sub_low, in_corner[2, i], in_corner[0, i]),
            )

    fixed = (bed, fric, qe, qs)
    stage(fixed, st_rows, st_cols)
    st_start, st_wait, st_done = edges(
        st_rows, st_cols, st_in_rows, st_in_cols, st_in_corner, st_s, st_r
    )
    st_start()

    for d in range(ny):
        place_t[d] = hit[d * cap : (d + 1) * cap].T.astype(jnp.bfloat16)

    from_all(take_idx, give_idx, idx_s, idx_r)
    for d in range(ny):
        target = lax.broadcasted_iota(jnp.int32, (land, cap), 0).astype(jnp.float32)
        target = (target == take_idx[d, 0:1]).astype(jnp.float32)
        where_to[d] = target.astype(jnp.bfloat16)
        where_to_t[d] = target.T.astype(jnp.bfloat16)

    st_wait()
    unstage(fixed, st_in_rows, st_in_cols, st_in_corner)
    b, fr = bed[...], fric[...]
    b_e, f_e, b_s, f_s = east_of(b), east_of(fr), south_of(b), south_of(fr)
    half = 0.5 * GRAVITY * TIME_STEP
    base_e[...] = jnp.maximum(b, b_e)
    base_s[...] = jnp.maximum(b, b_s)
    coef_e[...] = jnp.where((fr > 0.0) & (f_e > 0.0), half * (fr + f_e), -1.0)
    coef_s[...] = jnp.where((fr > 0.0) & (f_s > 0.0), half * (fr + f_s), -1.0)

    loads[9].wait()
    inflow = pick(where_to[gy], give[gy])
    for k in offsets(ny):
        peer = receive(take, give, give_s, give_r, k)
        inflow = inflow + pick(where_to[peer], take[peer])
    for c in range(chunks):
        at = (pl.ds(0, tr), pl.ds(c * LANES, LANES))
        h[at] = h[at] + inflow[c * tr : (c + 1) * tr]

    stage((h,), h_rows, h_cols)
    h_start, h_wait, h_done = edges(
        h_rows, h_cols, h_in_rows, h_in_cols, h_in_corner, hs_s, hs_r
    )
    h_start()
    h_wait()
    unstage((h,), h_in_rows, h_in_cols, h_in_corner)

    for step in range(SUB):
        eta = h[...] + bed[...]
        e = face(eta, east_of(eta), base_e[...], coef_e[...], qe[...])
        s = face(eta, south_of(eta), base_s[...], coef_s[...], qs[...])
        qe[...] = e
        qs[...] = s
        h[...] = h[...] + (TIME_STEP / CELL_WIDTH) * (
            pltpu.roll(e, 1, 1) - e + pltpu.roll(s, 1, 0) - s
        )

    blocks = jnp.concatenate(
        [h[0:tr, c * LANES : (c + 1) * LANES] for c in range(chunks)], axis=0
    )
    blocks = split3(blocks)
    for k in offsets(ny):
        peer = to_peer(k)
        give_lev[peer] = pick(where_to_t[peer], blocks)
        sent.append(send(give_lev, take_lev, lev_s, lev_r, k))
    mine = pick(place_t[gy], pick(where_to_t[gy], blocks))
    for k in offsets(ny):
        peer = receive(take_lev, give_lev, lev_s, lev_r, k)
        mine = mine + pick(place_t[peer], take_lev[peer])
    store = soil[...]
    runoff = rain[...] * store * store
    newsoil[...] = (
        store + rain[...] - runoff + INFIL_RATE * (1.0 - store) * (1.0 - jnp.exp(-mine))
    )
    for c in sent:
        c.wait_send()
    st_done()
    h_done()


def write_out(h, qe, qs, newsoil, depth_out, east_out, south_out, soil_out, sem):
    tr, tc = depth_out.shape
    inner = (pl.ds(0, tr), pl.ds(0, tc))
    copies = [
        pltpu.make_async_copy(src, dst, sem.at[i])
        for i, (src, dst) in enumerate(
            [
                (h.at[inner], depth_out), (qe.at[inner], east_out),
                (qs.at[inner], south_out), (newsoil, soil_out),
            ]
        )
    ]
    for c in copies:
        c.start()
    for c in copies:
        c.wait()


def local(depth, bed, east, south, rough, wet, soil, rain, column, block):
    nx, ny = lax.axis_size("gx"), lax.axis_size("gy")
    tr, tc = depth.shape
    land = soil.shape[1]
    cap = 2 * land // ny
    slots = ny * cap
    grid = (tr + EDGE, tc + LANES)
    f32, bf16, i32 = jnp.float32, jnp.bfloat16, jnp.int32
    v = pltpu.VMEM
    dma = pltpu.SemaphoreType.DMA
    peers = max(1, ny - 1)

    def edge_bufs(k):
        return [
            v((2, k, EDGE, tc), f32), v((2, k, EDGE, tr), f32),
            v((2, k, EDGE, tc), f32), v((2, k, EDGE, tr), f32), v((4, k, EDGE, LANES), f32),
        ]

    any_ = pl.BlockSpec(memory_space=pltpu.MemorySpace.HBM)
    vmem = pl.BlockSpec(memory_space=pltpu.VMEM)
    shape = jax.ShapeDtypeStruct
    out = pl.pallas_call(
        functools.partial(kernel, nx, ny, cap),
        out_shape=[shape(grid, f32)] * 3 + [shape((land, LANES), f32)],
        in_specs=[any_] * 10,
        out_specs=[vmem] * 4,
        scratch_shapes=[v(grid, f32)] * 2
        + [v((tr, tc), i32)] * 2
        + [v((land, LANES), f32)] * 2
        + [v((1, land), i32)] * 2
        + [v(grid, f32)] * 4
        + [v((ny, cap, LANES), f32)] * 2
        + [v((ny, EDGE, cap), f32)] * 2
        + [v((ny, cap, LANES), f32)] * 2
        + edge_bufs(4)
        + edge_bufs(1)
        + [v((slots, land), bf16), v((ny, land, cap), bf16)]
        + [v((ny, land, cap), bf16), v((ny, cap, land), bf16)]
        + [dma((10,))]
        + [dma((peers,))] * 6
        + [dma((8,))] * 4,
        compiler_params=pltpu.CompilerParams(collective_id=0, has_side_effects=True, vmem_limit_bytes=24 << 20
        ),
    )(
        *(
            pltpu.with_memory_space_constraint(x, pltpu.MemorySpace.HBM)
            for x in (
                depth, bed, east, south, rough, wet, soil[0], rain[0],
                column.reshape(1, land), block,
            )
        )
    )
    out = pl.pallas_call(
        write_out,
        out_shape=[shape((tr, tc), f32)] * 3 + [shape((land, LANES), f32)],
        in_specs=[vmem] * 4,
        out_specs=[any_] * 4,
        scratch_shapes=[dma((4,))],
        compiler_params=pltpu.CompilerParams(vmem_limit_bytes=8 << 20),
    )(*out)
    return out[0], out[1], out[2], out[3][None]


def solution(mesh):
    grid = P("gx", "gy")
    blocks = P("gx", "gy", None)
    return jax.shard_map(
        local, mesh=mesh,
        in_specs=(grid,) * 6 + (blocks,) * 3 + (grid,),
        out_specs=(grid,) * 3 + (blocks,),
        check_vma=False,
    )
```

```python
import functools

import jax
import jax.numpy as jnp
from jax import lax
from jax.experimental import pallas as pl
from jax.experimental.pallas import tpu as pltpu
from jax.sharding import PartitionSpec as P

SUB = 4
GRAVITY = 9.81
TIME_STEP = 1.0
CELL_WIDTH = 30.0
DEPTH_FLOOR = 0.3
INFIL_RATE = 0.5
MANNING = (0.02, 0.03, 0.035, 0.045, 0.06, 0.08, 0.1, 0.15)
LANES = 128
EDGE = 8
MESH = pl.DeviceIdType.MESH
AROUND = ((-1, -1), (-1, 0), (-1, 1), (0, -1), (0, 1), (1, -1), (1, 0), (1, 1))
NW, N, NE, W, E, SW, S, SE = range(8)


def split3(x):
    a = x.astype(jnp.bfloat16)
    rest = x - a.astype(jnp.float32)
    b = rest.astype(jnp.bfloat16)
    c = (rest - b.astype(jnp.float32)).astype(jnp.bfloat16)
    return jnp.concatenate([a, b, c], axis=1)


def pick(mask, x):
    x = x if x.dtype == jnp.bfloat16 else split3(x)
    y = jnp.dot(mask, x, preferred_element_type=jnp.float32)
    return y[:, :LANES] + y[:, LANES : 2 * LANES] + y[:, 2 * LANES :]


def flip(i, k, n):
    if n & (n - 1):
        return None
    both, bit = 0, 1
    while bit < n:
        if k & bit:
            both = both + bit * lax.rem(i // bit, 2)
        bit *= 2
    return i + k - 2 * both


def offsets(n):
    return sorted(range(1, n), key=lambda k: bin(k).count("1"))


def east_of(x):
    return pltpu.roll(x, x.shape[1] - 1, 1)


def south_of(x):
    return pltpu.roll(x, x.shape[0] - 1, 0)


def face(eta, eta_next, base, coef, q):
    depth = jnp.maximum(eta, eta_next) - base
    driving = (GRAVITY * TIME_STEP / CELL_WIDTH) * jnp.maximum(depth, 0.0) * (eta_next - eta)
    power = jnp.exp2(jnp.log2(jnp.maximum(depth, DEPTH_FLOOR)) * (-7.0 / 3.0))
    damping = 1.0 + coef * jnp.abs(q) * power
    return jnp.where(coef > 0.0, (q - driving) / damping, 0.0)


def kernel(
    nx, ny, cap,
    depth_in, bed_in, east_in, south_in, rough_in, wet_in, soil_in, rain_in, col_in, blk_in,
    h, qe, qs, newsoil,
    bed, fric, rough, wet, soil, rain, col, blk,
    base_e, base_s, coef_e, coef_s,
    give, take, give_idx, take_idx, give_lev, take_lev,
    st_rows, st_cols, st_in_rows, st_in_cols, st_in_corner,
    h_rows, h_cols, h_in_rows, h_in_cols, h_in_corner,
    place, place_t, where_to, where_to_t,
    in_sem, give_s, give_r, idx_s, idx_r, lev_s, lev_r, st_s, st_r, hs_s, hs_r,
):
    gx, gy = lax.axis_index("gx"), lax.axis_index("gy")
    tr, tc = rough.shape
    land = soil.shape[0]
    chunks = tc // LANES

    inner = (pl.ds(0, tr), pl.ds(0, tc))
    loads = [
        pltpu.make_async_copy(src, dst, in_sem.at[i])
        for i, (src, dst) in enumerate(
            [
                (col_in, col), (blk_in, blk), (soil_in, soil), (rain_in, rain),
                (rough_in, rough), (wet_in, wet), (bed_in, bed.at[inner]),
                (east_in, qe.at[inner]), (south_in, qs.at[inner]), (depth_in, h.at[inner]),
            ]
        )
    ]
    for c in loads:
        c.start()

    def there(k):
        dx, dy = AROUND[k]
        x, y = gx + dx, gy + dy
        return (x >= 0) & (x < nx) & (y >= 0) & (y < ny)

    barrier = pltpu.get_barrier_semaphore()
    for k in range(1, ny):
        pl.semaphore_signal(
            barrier, inc=1, device_id=(gx, lax.rem(gy + k, ny)), device_id_type=MESH
        )
    total = ny - 1
    for k in (NW, N, NE, SW, S, SE):
        dx, dy = AROUND[k]

        @pl.when(there(k))
        def _(dx=dx, dy=dy):
            pl.semaphore_signal(barrier, inc=1, device_id=(gx + dx, gy + dy), device_id_type=MESH)

        total = total + there(k).astype(jnp.int32)

    for k, ref in ((N, (st_in_rows, h_in_rows)), (S, (st_in_rows, h_in_rows))):
        @pl.when(jnp.logical_not(there(k)))
        def _(k=k, ref=ref):
            for r in ref:
                r[int(k == S)] = jnp.zeros(r.shape[1:], r.dtype)
    for k, ref in ((W, (st_in_cols, h_in_cols)), (E, (st_in_cols, h_in_cols))):
        @pl.when(jnp.logical_not(there(k)))
        def _(k=k, ref=ref):
            for r in ref:
                r[int(k == E)] = jnp.zeros(r.shape[1:], r.dtype)
    for n, k in enumerate((NW, NE, SW, SE)):
        @pl.when(jnp.logical_not(there(k)))
        def _(n=n):
            for r in (st_in_corner, h_in_corner):
                r[n] = jnp.zeros(r.shape[1:], r.dtype)

    loads[0].wait()
    loads[1].wait()
    column = col[...]
    groups = max(EDGE, ny)
    is_col = lax.broadcasted_iota(jnp.int32, (groups, land), 0) == column
    before = lax.broadcasted_iota(jnp.int32, (land, land), 0) < lax.broadcasted_iota(
        jnp.int32, (land, land), 1
    )
    rank = jnp.dot(
        is_col.astype(jnp.float32).astype(jnp.bfloat16),
        before.astype(jnp.float32).astype(jnp.bfloat16),
        preferred_element_type=jnp.float32,
    )
    rank = jnp.sum(jnp.where(is_col, rank, 0.0), axis=0, keepdims=True)
    slot = column.astype(jnp.float32) * cap + rank
    slots = ny * cap
    hit = lax.broadcasted_iota(jnp.int32, (slots, land), 0).astype(jnp.float32) == slot
    hit = hit.astype(jnp.float32)
    place[...] = hit.astype(jnp.bfloat16)

    block = blk[...].astype(jnp.float32)
    row = jnp.floor((block + 0.5) * (1.0 / chunks))
    chunk = block - row * chunks
    line = lax.broadcasted_iota(jnp.int32, (EDGE, land), 0)
    code = jnp.where(line == 0, row + 1.0, jnp.where(line == 1, chunk, 0.0))
    code = lax.dot_general(
        code.astype(jnp.bfloat16), place[...], (((1,), (1,)), ((), ())),
        preferred_element_type=jnp.float32,
    )
    owner = jnp.broadcast_to(code[1:2] * tr + code[0:1] - 1.0, (EDGE, slots))
    for d in range(ny):
        give_idx[d] = owner[:, d * cap : (d + 1) * cap]

    loads[2].wait()
    loads[3].wait()
    runoff = rain[...] * soil[...] * soil[...]
    packed = pick(place[...], runoff)
    for d in range(ny):
        give[d] = packed[d * cap : (d + 1) * cap]

    pl.semaphore_wait(barrier, total)

    def to_peer(k):
        peer = flip(gy, k, ny)
        return lax.rem(gy + k, ny) if peer is None else peer

    def from_peer(k):
        peer = flip(gy, k, ny)
        return lax.rem(gy + ny - k, ny) if peer is None else peer

    def send(src, dst, ss, rs, k):
        peer = to_peer(k)
        c = pltpu.make_async_remote_copy(
            src_ref=src.at[peer], dst_ref=dst.at[gy], send_sem=ss.at[k - 1],
            recv_sem=rs.at[k - 1], device_id=(gx, peer), device_id_type=MESH,
        )
        c.start()
        return c

    def to_all(src, dst, ss, rs):
        return [send(src, dst, ss, rs, k) for k in offsets(ny)]

    def receive(dst, src, ss, rs, k):
        peer = from_peer(k)
        pltpu.make_async_remote_copy(
            src_ref=src.at[peer], dst_ref=dst.at[peer], send_sem=ss.at[k - 1],
            recv_sem=rs.at[k - 1], device_id=(gx, peer), device_id_type=MESH,
        ).wait_recv()
        return peer

    def from_all(dst, src, ss, rs):
        for k in offsets(ny):
            receive(dst, src, ss, rs, k)

    sent = to_all(give_idx, take_idx, idx_s, idx_r)
    sent += to_all(give, take, give_s, give_r)
    take_idx[pl.ds(gy, 1)] = give_idx[pl.ds(gy, 1)]

    for i in range(4, 9):
        loads[i].wait()
    kind = rough[...]
    f = jnp.zeros((tr, tc), jnp.float32)
    for i, coefficient in enumerate(MANNING):
        f = jnp.where(kind == i, coefficient * coefficient, f)
    fric[inner] = jnp.where(wet[...] > 0, f, -1.0)
    lane_low = lax.broadcasted_iota(jnp.int32, (tr, LANES), 1) < LANES // 2

    def stage(fields, rows, cols):
        for i, ref in enumerate(fields):
            rows[0, i] = ref[0:EDGE, 0:tc]
            rows[1, i] = ref[tr - EDGE : tr, 0:tc]
            ends = jnp.where(lane_low, ref[0:tr, 0:LANES], ref[0:tr, tc - LANES : tc]).T
            cols[0, i] = ends[0:EDGE]
            cols[1, i] = ends[LANES - EDGE :]

    def edges(rows, cols, in_rows, in_cols, in_corner, ss, rs):
        first, last = pl.ds(0, LANES), pl.ds(tc - LANES, LANES)

        def piece(k):
            dx, dy = AROUND[k]
            if dy == 0:
                return rows.at[int(dx > 0)], in_rows.at[int(dx < 0)]
            if dx == 0:
                return cols.at[int(dy > 0)], in_cols.at[int(dy < 0)]
            side = last if dy > 0 else first
            corner = {NW: 3, NE: 2, SW: 1, SE: 0}[k]
            return rows.at[int(dx > 0), :, :, side], in_corner.at[corner]

        def copy(k):
            dx, dy = AROUND[k]
            src, dst = piece(k)
            return pltpu.make_async_remote_copy(
                src_ref=src, dst_ref=dst, send_sem=ss.at[k], recv_sem=rs.at[7 - k],
                device_id=(gx + dx, gy + dy), device_id_type=MESH,
            )

        def start():
            for k in (NW, NE, SW, SE, W, E, N, S):
                @pl.when(there(k))
                def _(k=k):
                    copy(k).start()

        def wait_recv():
            for k in range(8):
                @pl.when(there(k))
                def _(k=k):
                    copy(7 - k).wait_recv()

        def wait_send():
            for k in range(8):
                @pl.when(there(k))
                def _(k=k):
                    copy(k).wait_send()

        return start, wait_recv, wait_send

    sub_low = lax.broadcasted_iota(jnp.int32, (EDGE, 1), 0) < EDGE // 2

    def unstage(fields, in_rows, in_cols, in_corner):
        for i, ref in enumerate(fields):
            ref[tr : tr + EDGE, 0:tc] = jnp.where(sub_low, in_rows[1, i], in_rows[0, i])
            side = jnp.concatenate(
                [in_cols[1, i], jnp.zeros((LANES - 2 * EDGE, tr), jnp.float32), in_cols[0, i]],
                axis=0,
            )
            ref[0:tr, tc : tc + LANES] = side.T
            ref[tr : tr + EDGE, tc : tc + LANES] = jnp.where(
                lane_low[:EDGE],
                jnp.where(sub_low, in_corner[3, i], in_corner[1, i]),
                jnp.where(sub_low, in_corner[2, i], in_corner[0, i]),
            )

    fixed = (bed, fric, qe, qs)
    stage(fixed, st_rows, st_cols)
    st_start, st_wait, st_done = edges(
        st_rows, st_cols, st_in_rows, st_in_cols, st_in_corner, st_s, st_r
    )
    st_start()

    for d in range(ny):
        place_t[d] = hit[d * cap : (d + 1) * cap].T.astype(jnp.bfloat16)

    from_all(take_idx, give_idx, idx_s, idx_r)
    for d in range(ny):
        target = lax.broadcasted_iota(jnp.int32, (land, cap), 0).astype(jnp.float32)
        target = (target == take_idx[d, 0:1]).astype(jnp.float32)
        where_to[d] = target.astype(jnp.bfloat16)
        where_to_t[d] = target.T.astype(jnp.bfloat16)

    loads[9].wait()
    inflow = pick(where_to[gy], give[gy])
    for k in offsets(ny):
        peer = receive(take, give, give_s, give_r, k)
        inflow = inflow + pick(where_to[peer], take[peer])
    for c in range(chunks):
        at = (pl.ds(0, tr), pl.ds(c * LANES, LANES))
        h[at] = h[at] + inflow[c * tr : (c + 1) * tr]

    stage((h,), h_rows, h_cols)
    h_start, h_wait, h_done = edges(
        h_rows, h_cols, h_in_rows, h_in_cols, h_in_corner, hs_s, hs_r
    )
    h_start()

    st_wait()
    unstage(fixed, st_in_rows, st_in_cols, st_in_corner)
    b, fr = bed[...], fric[...]
    b_e, f_e, b_s, f_s = east_of(b), east_of(fr), south_of(b), south_of(fr)
    half = 0.5 * GRAVITY * TIME_STEP
    base_e[...] = jnp.maximum(b, b_e)
    base_s[...] = jnp.maximum(b, b_s)
    coef_e[...] = jnp.where((fr > 0.0) & (f_e > 0.0), half * (fr + f_e), -1.0)
    coef_s[...] = jnp.where((fr > 0.0) & (f_s > 0.0), half * (fr + f_s), -1.0)

    h_wait()
    unstage((h,), h_in_rows, h_in_cols, h_in_corner)

    for step in range(SUB):
        eta = h[...] + bed[...]
        e = face(eta, east_of(eta), base_e[...], coef_e[...], qe[...])
        s = face(eta, south_of(eta), base_s[...], coef_s[...], qs[...])
        qe[...] = e
        qs[...] = s
        h[...] = h[...] + (TIME_STEP / CELL_WIDTH) * (
            pltpu.roll(e, 1, 1) - e + pltpu.roll(s, 1, 0) - s
        )

    blocks = jnp.concatenate(
        [h[0:tr, c * LANES : (c + 1) * LANES] for c in range(chunks)], axis=0
    )
    blocks = split3(blocks)
    for k in offsets(ny):
        peer = to_peer(k)
        give_lev[peer] = pick(where_to_t[peer], blocks)
        sent.append(send(give_lev, take_lev, lev_s, lev_r, k))
    mine = pick(place_t[gy], pick(where_to_t[gy], blocks))
    for k in offsets(ny):
        peer = receive(take_lev, give_lev, lev_s, lev_r, k)
        mine = mine + pick(place_t[peer], take_lev[peer])
    store = soil[...]
    runoff = rain[...] * store * store
    newsoil[...] = (
        store + rain[...] - runoff + INFIL_RATE * (1.0 - store) * (1.0 - jnp.exp(-mine))
    )
    for c in sent:
        c.wait_send()
    st_done()
    h_done()


def write_out(h, qe, qs, newsoil, depth_out, east_out, south_out, soil_out, sem):
    tr, tc = depth_out.shape
    inner = (pl.ds(0, tr), pl.ds(0, tc))
    copies = [
        pltpu.make_async_copy(src, dst, sem.at[i])
        for i, (src, dst) in enumerate(
            [
                (h.at[inner], depth_out), (qe.at[inner], east_out),
                (qs.at[inner], south_out), (newsoil, soil_out),
            ]
        )
    ]
    for c in copies:
        c.start()
    for c in copies:
        c.wait()


def local(depth, bed, east, south, rough, wet, soil, rain, column, block):
    nx, ny = lax.axis_size("gx"), lax.axis_size("gy")
    tr, tc = depth.shape
    land = soil.shape[1]
    cap = 2 * land // ny
    slots = ny * cap
    grid = (tr + EDGE, tc + LANES)
    f32, bf16, i32 = jnp.float32, jnp.bfloat16, jnp.int32
    v = pltpu.VMEM
    dma = pltpu.SemaphoreType.DMA
    peers = max(1, ny - 1)

    def edge_bufs(k):
        return [
            v((2, k, EDGE, tc), f32), v((2, k, EDGE, tr), f32),
            v((2, k, EDGE, tc), f32), v((2, k, EDGE, tr), f32), v((4, k, EDGE, LANES), f32),
        ]

    any_ = pl.BlockSpec(memory_space=pltpu.MemorySpace.HBM)
    vmem = pl.BlockSpec(memory_space=pltpu.VMEM)
    shape = jax.ShapeDtypeStruct
    out = pl.pallas_call(
        functools.partial(kernel, nx, ny, cap),
        out_shape=[shape(grid, f32)] * 3 + [shape((land, LANES), f32)],
        in_specs=[any_] * 10,
        out_specs=[vmem] * 4,
        scratch_shapes=[v(grid, f32)] * 2
        + [v((tr, tc), i32)] * 2
        + [v((land, LANES), f32)] * 2
        + [v((1, land), i32)] * 2
        + [v(grid, f32)] * 4
        + [v((ny, cap, LANES), f32)] * 2
        + [v((ny, EDGE, cap), f32)] * 2
        + [v((ny, cap, LANES), f32)] * 2
        + edge_bufs(4)
        + edge_bufs(1)
        + [v((slots, land), bf16), v((ny, land, cap), bf16)]
        + [v((ny, land, cap), bf16), v((ny, cap, land), bf16)]
        + [dma((10,))]
        + [dma((peers,))] * 6
        + [dma((8,))] * 4,
        compiler_params=pltpu.CompilerParams(collective_id=0, has_side_effects=True, vmem_limit_bytes=24 << 20
        ),
    )(
        *(
            pltpu.with_memory_space_constraint(x, pltpu.MemorySpace.HBM)
            for x in (
                depth, bed, east, south, rough, wet, soil[0], rain[0],
                column.reshape(1, land), block,
            )
        )
    )
    out = pl.pallas_call(
        write_out,
        out_shape=[shape((tr, tc), f32)] * 3 + [shape((land, LANES), f32)],
        in_specs=[vmem] * 4,
        out_specs=[any_] * 4,
        scratch_shapes=[dma((4,))],
        compiler_params=pltpu.CompilerParams(vmem_limit_bytes=8 << 20),
    )(*out)
    return out[0], out[1], out[2], out[3][None]


def solution(mesh):
    grid = P("gx", "gy")
    blocks = P("gx", "gy", None)
    return jax.shard_map(
        local, mesh=mesh,
        in_specs=(grid,) * 6 + (blocks,) * 3 + (grid,),
        out_specs=(grid,) * 3 + (blocks,),
        check_vma=False,
    )
```

```python
import functools

import jax
import jax.numpy as jnp
from jax import lax
from jax.experimental import pallas as pl
from jax.experimental.pallas import tpu as pltpu
from jax.sharding import PartitionSpec as P

SUB = 4
GRAVITY = 9.81
TIME_STEP = 1.0
CELL_WIDTH = 30.0
DEPTH_FLOOR = 0.3
INFIL_RATE = 0.5
MANNING = (0.02, 0.03, 0.035, 0.045, 0.06, 0.08, 0.1, 0.15)
LANES = 128
EDGE = 8
MESH = pl.DeviceIdType.MESH
AROUND = ((-1, -1), (-1, 0), (-1, 1), (0, -1), (0, 1), (1, -1), (1, 0), (1, 1))
NW, N, NE, W, E, SW, S, SE = range(8)


def split3(x):
    a = x.astype(jnp.bfloat16)
    rest = x - a.astype(jnp.float32)
    b = rest.astype(jnp.bfloat16)
    c = (rest - b.astype(jnp.float32)).astype(jnp.bfloat16)
    return jnp.concatenate([a, b, c], axis=1)


def pick(mask, x):
    x = x if x.dtype == jnp.bfloat16 else split3(x)
    y = jnp.dot(mask, x, preferred_element_type=jnp.float32)
    return y[:, :LANES] + y[:, LANES : 2 * LANES] + y[:, 2 * LANES :]


def flip(i, k, n):
    if n & (n - 1):
        return None
    both, bit = 0, 1
    while bit < n:
        if k & bit:
            both = both + bit * lax.rem(i // bit, 2)
        bit *= 2
    return i + k - 2 * both


def offsets(n):
    return sorted(range(1, n), key=lambda k: bin(k).count("1"))


def east_of(x):
    return pltpu.roll(x, x.shape[1] - 1, 1)


def south_of(x):
    return pltpu.roll(x, x.shape[0] - 1, 0)


def face(eta, eta_next, base, coef, q):
    depth = jnp.maximum(eta, eta_next) - base
    driving = (GRAVITY * TIME_STEP / CELL_WIDTH) * jnp.maximum(depth, 0.0) * (eta_next - eta)
    power = jnp.exp2(jnp.log2(jnp.maximum(depth, DEPTH_FLOOR)) * (-7.0 / 3.0))
    damping = 1.0 + coef * jnp.abs(q) * power
    return jnp.where(coef > 0.0, (q - driving) / damping, 0.0)


def kernel(
    nx, ny, cap,
    depth_in, bed_in, east_in, south_in, rough_in, wet_in, soil_in, rain_in, col_in, blk_in,
    h, qe, qs, newsoil,
    bed, fric, rough, wet, soil, rain, col, blk,
    base_e, base_s, coef_e, coef_s,
    give, take, give_idx, take_idx, give_lev, take_lev,
    st_rows, st_cols, st_in_rows, st_in_cols, st_in_corner,
    h_rows, h_cols, h_in_rows, h_in_cols, h_in_corner,
    place, place_t, where_to, where_to_t,
    in_sem, give_s, give_r, idx_s, idx_r, lev_s, lev_r, st_s, st_r, hs_s, hs_r,
):
    gx, gy = lax.axis_index("gx"), lax.axis_index("gy")
    tr, tc = rough.shape
    land = soil.shape[0]
    chunks = tc // LANES

    inner = (pl.ds(0, tr), pl.ds(0, tc))
    loads = [
        pltpu.make_async_copy(src, dst, in_sem.at[i])
        for i, (src, dst) in enumerate(
            [
                (col_in, col), (blk_in, blk), (soil_in, soil), (rain_in, rain),
                (rough_in, rough), (wet_in, wet), (bed_in, bed.at[inner]),
                (east_in, qe.at[inner]), (south_in, qs.at[inner]), (depth_in, h.at[inner]),
            ]
        )
    ]
    for c in loads:
        c.start()

    def there(k):
        dx, dy = AROUND[k]
        x, y = gx + dx, gy + dy
        return (x >= 0) & (x < nx) & (y >= 0) & (y < ny)

    barrier = pltpu.get_barrier_semaphore()
    for k in range(1, ny):
        pl.semaphore_signal(
            barrier, inc=1, device_id=(gx, lax.rem(gy + k, ny)), device_id_type=MESH
        )
    total = ny - 1
    for k in (NW, N, NE, SW, S, SE):
        dx, dy = AROUND[k]

        @pl.when(there(k))
        def _(dx=dx, dy=dy):
            pl.semaphore_signal(barrier, inc=1, device_id=(gx + dx, gy + dy), device_id_type=MESH)

        total = total + there(k).astype(jnp.int32)

    for k, ref in ((N, (st_in_rows, h_in_rows)), (S, (st_in_rows, h_in_rows))):
        @pl.when(jnp.logical_not(there(k)))
        def _(k=k, ref=ref):
            for r in ref:
                r[int(k == S)] = jnp.zeros(r.shape[1:], r.dtype)
    for k, ref in ((W, (st_in_cols, h_in_cols)), (E, (st_in_cols, h_in_cols))):
        @pl.when(jnp.logical_not(there(k)))
        def _(k=k, ref=ref):
            for r in ref:
                r[int(k == E)] = jnp.zeros(r.shape[1:], r.dtype)
    for n, k in enumerate((NW, NE, SW, SE)):
        @pl.when(jnp.logical_not(there(k)))
        def _(n=n):
            for r in (st_in_corner, h_in_corner):
                r[n] = jnp.zeros(r.shape[1:], r.dtype)

    loads[0].wait()
    loads[1].wait()
    column = col[...]
    groups = max(EDGE, ny)
    is_col = lax.broadcasted_iota(jnp.int32, (groups, land), 0) == column
    before = lax.broadcasted_iota(jnp.int32, (land, land), 0) < lax.broadcasted_iota(
        jnp.int32, (land, land), 1
    )
    rank = jnp.dot(
        is_col.astype(jnp.float32).astype(jnp.bfloat16),
        before.astype(jnp.float32).astype(jnp.bfloat16),
        preferred_element_type=jnp.float32,
    )
    rank = jnp.sum(jnp.where(is_col, rank, 0.0), axis=0, keepdims=True)
    slot = column.astype(jnp.float32) * cap + rank
    slots = ny * cap
    hit = lax.broadcasted_iota(jnp.int32, (slots, land), 0).astype(jnp.float32) == slot
    hit = hit.astype(jnp.float32)
    place[...] = hit.astype(jnp.bfloat16)

    block = blk[...].astype(jnp.float32)
    row = jnp.floor((block + 0.5) * (1.0 / chunks))
    chunk = block - row * chunks
    line = lax.broadcasted_iota(jnp.int32, (EDGE, land), 0)
    code = jnp.where(line == 0, row + 1.0, jnp.where(line == 1, chunk, 0.0))
    code = lax.dot_general(
        code.astype(jnp.bfloat16), place[...], (((1,), (1,)), ((), ())),
        preferred_element_type=jnp.float32,
    )
    owner = jnp.broadcast_to(code[1:2] * tr + code[0:1] - 1.0, (EDGE, slots))
    for d in range(ny):
        give_idx[d] = owner[:, d * cap : (d + 1) * cap]

    loads[2].wait()
    loads[3].wait()
    runoff = rain[...] * soil[...] * soil[...]
    packed = pick(place[...], runoff)
    for d in range(ny):
        give[d] = packed[d * cap : (d + 1) * cap]

    pl.semaphore_wait(barrier, total)

    def to_peer(k):
        peer = flip(gy, k, ny)
        return lax.rem(gy + k, ny) if peer is None else peer

    def from_peer(k):
        peer = flip(gy, k, ny)
        return lax.rem(gy + ny - k, ny) if peer is None else peer

    def send(src, dst, ss, rs, k):
        peer = to_peer(k)
        c = pltpu.make_async_remote_copy(
            src_ref=src.at[peer], dst_ref=dst.at[gy], send_sem=ss.at[k - 1],
            recv_sem=rs.at[k - 1], device_id=(gx, peer), device_id_type=MESH,
        )
        c.start()
        return c

    def to_all(src, dst, ss, rs):
        return [send(src, dst, ss, rs, k) for k in offsets(ny)]

    def receive(dst, src, ss, rs, k):
        peer = from_peer(k)
        pltpu.make_async_remote_copy(
            src_ref=src.at[peer], dst_ref=dst.at[peer], send_sem=ss.at[k - 1],
            recv_sem=rs.at[k - 1], device_id=(gx, peer), device_id_type=MESH,
        ).wait_recv()
        return peer

    def from_all(dst, src, ss, rs):
        for k in offsets(ny):
            receive(dst, src, ss, rs, k)

    sent = to_all(give_idx, take_idx, idx_s, idx_r)
    sent += to_all(give, take, give_s, give_r)
    take_idx[pl.ds(gy, 1)] = give_idx[pl.ds(gy, 1)]

    for i in range(4, 9):
        loads[i].wait()
    kind = rough[...]
    f = jnp.zeros((tr, tc), jnp.float32)
    for i, coefficient in enumerate(MANNING):
        f = jnp.where(kind == i, coefficient * coefficient, f)
    fric[inner] = jnp.where(wet[...] > 0, f, -1.0)
    lane_low = lax.broadcasted_iota(jnp.int32, (tr, LANES), 1) < LANES // 2

    def stage(fields, rows, cols):
        for i, ref in enumerate(fields):
            rows[0, i] = ref[0:EDGE, 0:tc]
            rows[1, i] = ref[tr - EDGE : tr, 0:tc]
            ends = jnp.where(lane_low, ref[0:tr, 0:LANES], ref[0:tr, tc - LANES : tc]).T
            cols[0, i] = ends[0:EDGE]
            cols[1, i] = ends[LANES - EDGE :]

    def edges(rows, cols, in_rows, in_cols, in_corner, ss, rs):
        first, last = pl.ds(0, LANES), pl.ds(tc - LANES, LANES)

        def piece(k):
            dx, dy = AROUND[k]
            if dy == 0:
                return rows.at[int(dx > 0)], in_rows.at[int(dx < 0)]
            if dx == 0:
                return cols.at[int(dy > 0)], in_cols.at[int(dy < 0)]
            side = last if dy > 0 else first
            corner = {NW: 3, NE: 2, SW: 1, SE: 0}[k]
            return rows.at[int(dx > 0), :, :, side], in_corner.at[corner]

        def copy(k):
            dx, dy = AROUND[k]
            src, dst = piece(k)
            return pltpu.make_async_remote_copy(
                src_ref=src, dst_ref=dst, send_sem=ss.at[k], recv_sem=rs.at[7 - k],
                device_id=(gx + dx, gy + dy), device_id_type=MESH,
            )

        def start():
            for k in (NW, NE, SW, SE, W, E, N, S):
                @pl.when(there(k))
                def _(k=k):
                    copy(k).start()

        def wait_recv():
            for k in range(8):
                @pl.when(there(k))
                def _(k=k):
                    copy(7 - k).wait_recv()

        def wait_send():
            for k in range(8):
                @pl.when(there(k))
                def _(k=k):
                    copy(k).wait_send()

        return start, wait_recv, wait_send

    sub_low = lax.broadcasted_iota(jnp.int32, (EDGE, 1), 0) < EDGE // 2

    def unstage(fields, in_rows, in_cols, in_corner):
        for i, ref in enumerate(fields):
            ref[tr : tr + EDGE, 0:tc] = jnp.where(sub_low, in_rows[1, i], in_rows[0, i])
            side = jnp.concatenate(
                [in_cols[1, i], jnp.zeros((LANES - 2 * EDGE, tr), jnp.float32), in_cols[0, i]],
                axis=0,
            )
            ref[0:tr, tc : tc + LANES] = side.T
            ref[tr : tr + EDGE, tc : tc + LANES] = jnp.where(
                lane_low[:EDGE],
                jnp.where(sub_low, in_corner[3, i], in_corner[1, i]),
                jnp.where(sub_low, in_corner[2, i], in_corner[0, i]),
            )

    fixed = (bed, fric, qe, qs)
    stage(fixed, st_rows, st_cols)
    st_start, st_wait, st_done = edges(
        st_rows, st_cols, st_in_rows, st_in_cols, st_in_corner, st_s, st_r
    )

    for d in range(ny):
        place_t[d] = hit[d * cap : (d + 1) * cap].T.astype(jnp.bfloat16)

    from_all(take_idx, give_idx, idx_s, idx_r)
    for d in range(ny):
        target = lax.broadcasted_iota(jnp.int32, (land, cap), 0).astype(jnp.float32)
        target = (target == take_idx[d, 0:1]).astype(jnp.float32)
        where_to[d] = target.astype(jnp.bfloat16)
        where_to_t[d] = target.T.astype(jnp.bfloat16)

    st_start()
    loads[9].wait()
    inflow = pick(where_to[gy], give[gy])
    for k in offsets(ny):
        peer = receive(take, give, give_s, give_r, k)
        inflow = inflow + pick(where_to[peer], take[peer])
    for c in range(chunks):
        at = (pl.ds(0, tr), pl.ds(c * LANES, LANES))
        h[at] = h[at] + inflow[c * tr : (c + 1) * tr]

    stage((h,), h_rows, h_cols)
    h_start, h_wait, h_done = edges(
        h_rows, h_cols, h_in_rows, h_in_cols, h_in_corner, hs_s, hs_r
    )
    h_start()

    st_wait()
    unstage(fixed, st_in_rows, st_in_cols, st_in_corner)
    b, fr = bed[...], fric[...]
    b_e, f_e, b_s, f_s = east_of(b), east_of(fr), south_of(b), south_of(fr)
    half = 0.5 * GRAVITY * TIME_STEP
    base_e[...] = jnp.maximum(b, b_e)
    base_s[...] = jnp.maximum(b, b_s)
    coef_e[...] = jnp.where((fr > 0.0) & (f_e > 0.0), half * (fr + f_e), -1.0)
    coef_s[...] = jnp.where((fr > 0.0) & (f_s > 0.0), half * (fr + f_s), -1.0)

    h_wait()
    unstage((h,), h_in_rows, h_in_cols, h_in_corner)

    for step in range(SUB):
        eta = h[...] + bed[...]
        e = face(eta, east_of(eta), base_e[...], coef_e[...], qe[...])
        s = face(eta, south_of(eta), base_s[...], coef_s[...], qs[...])
        qe[...] = e
        qs[...] = s
        h[...] = h[...] + (TIME_STEP / CELL_WIDTH) * (
            pltpu.roll(e, 1, 1) - e + pltpu.roll(s, 1, 0) - s
        )

    blocks = jnp.concatenate(
        [h[0:tr, c * LANES : (c + 1) * LANES] for c in range(chunks)], axis=0
    )
    blocks = split3(blocks)
    for k in offsets(ny):
        peer = to_peer(k)
        give_lev[peer] = pick(where_to_t[peer], blocks)
        sent.append(send(give_lev, take_lev, lev_s, lev_r, k))
    mine = pick(place_t[gy], pick(where_to_t[gy], blocks))
    for k in offsets(ny):
        peer = receive(take_lev, give_lev, lev_s, lev_r, k)
        mine = mine + pick(place_t[peer], take_lev[peer])
    store = soil[...]
    runoff = rain[...] * store * store
    newsoil[...] = (
        store + rain[...] - runoff + INFIL_RATE * (1.0 - store) * (1.0 - jnp.exp(-mine))
    )
    for c in sent:
        c.wait_send()
    st_done()
    h_done()


def write_out(h, qe, qs, newsoil, depth_out, east_out, south_out, soil_out, sem):
    tr, tc = depth_out.shape
    inner = (pl.ds(0, tr), pl.ds(0, tc))
    copies = [
        pltpu.make_async_copy(src, dst, sem.at[i])
        for i, (src, dst) in enumerate(
            [
                (h.at[inner], depth_out), (qe.at[inner], east_out),
                (qs.at[inner], south_out), (newsoil, soil_out),
            ]
        )
    ]
    for c in copies:
        c.start()
    for c in copies:
        c.wait()


def local(depth, bed, east, south, rough, wet, soil, rain, column, block):
    nx, ny = lax.axis_size("gx"), lax.axis_size("gy")
    tr, tc = depth.shape
    land = soil.shape[1]
    cap = 2 * land // ny
    slots = ny * cap
    grid = (tr + EDGE, tc + LANES)
    f32, bf16, i32 = jnp.float32, jnp.bfloat16, jnp.int32
    v = pltpu.VMEM
    dma = pltpu.SemaphoreType.DMA
    peers = max(1, ny - 1)

    def edge_bufs(k):
        return [
            v((2, k, EDGE, tc), f32), v((2, k, EDGE, tr), f32),
            v((2, k, EDGE, tc), f32), v((2, k, EDGE, tr), f32), v((4, k, EDGE, LANES), f32),
        ]

    any_ = pl.BlockSpec(memory_space=pltpu.MemorySpace.HBM)
    vmem = pl.BlockSpec(memory_space=pltpu.VMEM)
    shape = jax.ShapeDtypeStruct
    out = pl.pallas_call(
        functools.partial(kernel, nx, ny, cap),
        out_shape=[shape(grid, f32)] * 3 + [shape((land, LANES), f32)],
        in_specs=[any_] * 10,
        out_specs=[vmem] * 4,
        scratch_shapes=[v(grid, f32)] * 2
        + [v((tr, tc), i32)] * 2
        + [v((land, LANES), f32)] * 2
        + [v((1, land), i32)] * 2
        + [v(grid, f32)] * 4
        + [v((ny, cap, LANES), f32)] * 2
        + [v((ny, EDGE, cap), f32)] * 2
        + [v((ny, cap, LANES), f32)] * 2
        + edge_bufs(4)
        + edge_bufs(1)
        + [v((slots, land), bf16), v((ny, land, cap), bf16)]
        + [v((ny, land, cap), bf16), v((ny, cap, land), bf16)]
        + [dma((10,))]
        + [dma((peers,))] * 6
        + [dma((8,))] * 4,
        compiler_params=pltpu.CompilerParams(collective_id=0, has_side_effects=True, vmem_limit_bytes=24 << 20
        ),
    )(
        *(
            pltpu.with_memory_space_constraint(x, pltpu.MemorySpace.HBM)
            for x in (
                depth, bed, east, south, rough, wet, soil[0], rain[0],
                column.reshape(1, land), block,
            )
        )
    )
    out = pl.pallas_call(
        write_out,
        out_shape=[shape((tr, tc), f32)] * 3 + [shape((land, LANES), f32)],
        in_specs=[vmem] * 4,
        out_specs=[any_] * 4,
        scratch_shapes=[dma((4,))],
        compiler_params=pltpu.CompilerParams(vmem_limit_bytes=8 << 20),
    )(*out)
    return out[0], out[1], out[2], out[3][None]


def solution(mesh):
    grid = P("gx", "gy")
    blocks = P("gx", "gy", None)
    return jax.shard_map(
        local, mesh=mesh,
        in_specs=(grid,) * 6 + (blocks,) * 3 + (grid,),
        out_specs=(grid,) * 3 + (blocks,),
        check_vma=False,
    )
```
